32 devices in a mesh: row: 8 (over y, x, core), col: 4 (over z).
Axes of the slice: x: 2, y: 2, z: 4, core: 2. Of those that a mesh axis runs over, the one named last changes fastest.
Arguments:
- layer_input: bfloat16 [256, 6144], P('row', 'col'), may hold values from -6 to 6
- norm_gain_rows: float32 [2, 6144], P(None, 'col'), may hold values from 0.1 to 1.9
- norm_bias_rows: float32 [2, 6144], P(None, 'col'), may hold values from -3 to 3
- query_key_value_weight: bfloat16 [6144, 3, 6144], P('col', None, 'row'), may hold values from -0.078125 to 0.078125
- adapter_down_maps: bfloat16 [64, 16, 6144], P(None, None, 'col'), may hold values from -0.078125 to 0.078125
- adapter_up_maps: bfloat16 [64, 16, 3, 6144], P(None, None, None, 'row'), may hold values from -6.5 to 6.5
- output_projection: bfloat16 [6144, 6144], P('row', 'col'), may hold values from -0.078125 to 0.078125
- up_projection: bfloat16 [6144, 24576], P('col', 'row'), may hold values from -0.078125 to 0.078125
- down_projection: bfloat16 [24576, 6144], P('row', 'col'), may hold values from -0.0390625 to 0.0390625
- prompt_token_length: int32 [4], replicated, may hold values from 1 to 64, 160 in all
- adapter_index: int32 [4], replicated, may hold values from 0 to 63
- prompt_page_map: int32 [4], replicated, may hold values from 0 to 3, each once
Outputs:
- new_hidden: bfloat16 [256, 6144], P('row', 'col')
- kv_pages: bfloat16 [4, 2, 64, 6144], P('col', None, None, 'row')
The draws below stay inside these ranges and needn't reach their ends.
Inputs may be any that keep to these rules, and one draw needn't show every extreme that they name: `prompt_page_map`: each page is named by exactly one prompt. `prompt_token_length`: the prompts together hold 4 * 64 * 5 // 8 real tokens; some prompt fills all 64 positions.
All inputs are finite; a program needn't handle non-finite values.
Results may differ from the reference program's by a relative error of at most 0.023.
Values may be sent and summed in bfloat16 or wider, within the bound.
A program may use at most 128 MiB of HBM per device.

```python
import math
import jax
import jax.numpy as jnp
import numpy as np
from jax import lax

MODEL_WIDTH = 6144
HEADS = 64
HD = 96
FF = 24576
ROT = 24
ADAPTER_RANK = 16
ADAPTER_COUNT = 64
PLEN = 64
PROMPT_COUNT = 4
TOKENS = 256
N_ROW = 8
N_COL = 4


def draw_layer_input(key, part):
    key_base = jax.random.fold_in(key, 11)
    normal_base = jnp.clip(jax.random.normal(key_base, (TOKENS, MODEL_WIDTH), jnp.float32), -6.0, 6.0)
    return normal_base.astype(jnp.bfloat16)


def draw_adapter_up_maps(key, part):
    key_base = jax.random.fold_in(key, 21)
    normal_base = jax.random.normal(key_base, (ADAPTER_COUNT, ADAPTER_RANK, 3, HEADS * HD), jnp.float32)
    result = jnp.clip(normal_base, -6.0, 6.0) * ADAPTER_RANK ** (-0.5)
    return result.astype(jnp.bfloat16)


def place_ends(array, stream_key, smallest, high):
    longest = array.shape.index(max(array.shape))
    spots = []
    for shift in (0, 1):
        where = [jax.random.randint(jax.random.fold_in(stream_key, axis), (), 0, length) for axis, length in enumerate(array.shape)]
        where[longest] = (where[longest] + shift) % array.shape[longest]
        spots.append(tuple(where))
    return array.at[spots[0]].set(smallest).at[spots[1]].set(high)


def steps_of(key, dims, cuts, least, high):
    level = 1.0
    for dim, blocks in cuts:
        steps = jax.random.uniform(jax.random.fold_in(jax.random.fold_in(key, 6), dim), (blocks,), jnp.float32, least / len(cuts), high / len(cuts))
        level = level * jnp.repeat(jnp.exp(steps), dims[dim] // blocks).reshape((-1,) + (1,) * (len(dims) - 1 - dim))
    return level


def split_up(number_of, total, most, skew):
    portions = [(1 << 20) // math.isqrt(grade ** skew) + 1 for grade in range(2, number_of + 1)]
    spare, counts = total - most - (number_of - 1), [1] * (number_of - 1)
    while spare > 0:
        free = [i for i in range(number_of - 1) if counts[i] < most]
        whole, budget = sum([portions[i] for i in free]), spare
        for i in free:
            addition = min(most - counts[i], max(1, budget * portions[i] // whole), spare)
            counts[i] = counts[i] + addition
            spare = spare - addition
    return np.array([most] + counts)


def uneven(stream_key, number_of, total, limit, slope):
    if number_of == 2:
        one = jax.random.randint(stream_key, (), max(1, total - limit), min(limit, total - 1) + 1)
        return jnp.stack([one, total - one])
    tallies = jnp.asarray(split_up(number_of, total, limit, slope), jnp.int32)
    pairs = (number_of - 1) // 2
    donor, taker = tallies[1:1 + 2 * pairs:2], tallies[2:2 + 2 * pairs:2]
    margin = jnp.minimum(donor - 1, limit - taker)
    moved = jax.random.randint(jax.random.fold_in(stream_key, 1), (pairs,), 0, 1 << 20) % (margin + 1)
    tallies = tallies.at[1:1 + 2 * pairs:2].set(donor - moved).at[2:2 + 2 * pairs:2].set(taker + moved)
    return tallies[jax.random.permutation(jax.random.fold_in(stream_key, 2), number_of)]


def gaussian(key, extent, width, most, shards=(), kind=jnp.bfloat16):
    values = width * jax.random.normal(key, extent, jnp.float32)
    if shards:
        values = values * steps_of(key, extent, shards, -0.22, 0.18)
    return jnp.clip(values, -most, most).astype(kind)


def setup_inputs(seed: int = 0) -> dict:
    seeds = jax.random.split(jax.random.key(seed), 13)
    layer_input = draw_layer_input(jax.random.fold_in(seeds[12], 71), 0)
    norm_gain_rows = jnp.clip(1.0 + 0.18 * jax.random.normal(seeds[1], (2, MODEL_WIDTH), jnp.float32), 0.1, 1.9)
    norm_bias_rows = gaussian(seeds[2], (2, MODEL_WIDTH), 0.5, 3.0, ((1, 4),), jnp.float32)
    query_key_value_weight = gaussian(seeds[3], (MODEL_WIDTH, 3, HEADS * HD), MODEL_WIDTH ** -0.5, 0.078125, ((0, 4), (2, 8)))
    adapter_down_maps = gaussian(seeds[4], (ADAPTER_COUNT, ADAPTER_RANK, MODEL_WIDTH), MODEL_WIDTH ** -0.5, 0.078125, ((2, 4),))
    adapter_up_maps = draw_adapter_up_maps(jax.random.fold_in(seeds[12], 71), 0)
    output_projection = gaussian(seeds[6], (HEADS * HD, MODEL_WIDTH), (HEADS * HD) ** -0.5, 0.078125, ((0, 8), (1, 4)))
    up_projection = gaussian(seeds[7], (MODEL_WIDTH, FF), MODEL_WIDTH ** -0.5, 0.078125, ((0, 4), (1, 8)))
    down_projection = gaussian(seeds[8], (FF, MODEL_WIDTH), FF ** -0.5, 0.0390625, ((0, 8), (1, 4)))
    prompt_token_length = uneven(seeds[9], PROMPT_COUNT, N_COL * PLEN * 5 // 8, PLEN, 2).astype(jnp.int32)
    adapter_index = place_ends(jax.random.randint(seeds[10], (PROMPT_COUNT,), 0, ADAPTER_COUNT), jax.random.fold_in(seeds[10], 1), 0, ADAPTER_COUNT - 1).astype(jnp.int32)
    prompt_page_map = jax.random.permutation(seeds[11], PROMPT_COUNT).astype(jnp.int32)
    return dict(layer_input=layer_input, norm_gain_rows=norm_gain_rows, norm_bias_rows=norm_bias_rows, query_key_value_weight=query_key_value_weight, adapter_down_maps=adapter_down_maps, adapter_up_maps=adapter_up_maps, output_projection=output_projection, up_projection=up_projection, down_projection=down_projection, prompt_token_length=prompt_token_length, adapter_index=adapter_index, prompt_page_map=prompt_page_map)


def norm_rows(hidden_f32, gain_row, bias_row):
    row_mean = lax.optimization_barrier(jnp.sum(hidden_f32, axis=-1, keepdims=True)) / MODEL_WIDTH
    row_var = lax.optimization_barrier(jnp.sum(hidden_f32 * hidden_f32, axis=-1, keepdims=True)) / MODEL_WIDTH - row_mean * row_mean
    return (hidden_f32 - row_mean) * lax.rsqrt(row_var + 1e-05) * gain_row + bias_row

def rotate(heads_in, positions):
    half_rot = ROT // 2
    inv_freq = 10000.0 ** (-jnp.arange(half_rot, dtype=jnp.float32) * 2.0 / ROT)
    angles = positions.astype(jnp.float32)[:, None] * inv_freq[None, :]
    cosine = jnp.cos(angles)[:, None, :]
    sine_part = jnp.sin(angles)[:, None, :]
    front_part = heads_in[..., :half_rot]
    back_part = heads_in[..., half_rot:ROT]
    return jnp.concatenate([front_part * cosine - back_part * sine_part, back_part * cosine + front_part * sine_part, heads_in[..., ROT:]], axis=-1)

def rounded(value):
    return lax.optimization_barrier(value.astype(jnp.bfloat16)).astype(jnp.float32)

def reference(layer_input, norm_gain_rows, norm_bias_rows, query_key_value_weight, adapter_down_maps, adapter_up_maps, output_projection, up_projection, down_projection, prompt_token_length, adapter_index, prompt_page_map):
    hidden_f32 = layer_input.astype(jnp.float32)
    normed_attn = norm_rows(hidden_f32, norm_gain_rows[0], norm_bias_rows[0]).astype(jnp.bfloat16)
    normed_mlp = norm_rows(hidden_f32, norm_gain_rows[1], norm_bias_rows[1]).astype(jnp.bfloat16)
    col_width = MODEL_WIDTH // N_COL
    query_key_value_width = 3 * HEADS * HD
    wide_weight = query_key_value_weight.reshape(MODEL_WIDTH, query_key_value_width)
    selected_down = adapter_down_maps[adapter_index]
    selected_up = adapter_up_maps[adapter_index].reshape(PROMPT_COUNT, ADAPTER_RANK, query_key_value_width)
    qkv_sum = jnp.zeros((TOKENS, query_key_value_width), jnp.float32)
    up_sum = jnp.zeros((TOKENS, FF), jnp.float32)
    for block_index in range(N_COL):
        low_col = block_index * col_width
        piece_attn = normed_attn[:, low_col:low_col + col_width]
        base_term = jnp.dot(piece_attn, wide_weight[low_col:low_col + col_width], preferred_element_type=jnp.float32)
        low_rank = jnp.einsum('pld,prd->plr', piece_attn.reshape(PROMPT_COUNT, PLEN, col_width).astype(jnp.float32), selected_down[:, :, low_col:low_col + col_width].astype(jnp.float32), precision=lax.Precision.HIGHEST).astype(jnp.bfloat16)
        extra_term = jnp.einsum('plr,prk->plk', low_rank.astype(jnp.float32), selected_up.astype(jnp.float32), precision=lax.Precision.HIGHEST).reshape(TOKENS, query_key_value_width)
        qkv_sum = qkv_sum + rounded(base_term + extra_term)
        piece_mlp = normed_mlp[:, low_col:low_col + col_width]
        up_sum = up_sum + rounded(jnp.dot(piece_mlp, up_projection[low_col:low_col + col_width], preferred_element_type=jnp.float32))
    hidden = jax.nn.gelu(up_sum, approximate=False).astype(jnp.bfloat16)
    qkv_sum = qkv_sum.reshape(PROMPT_COUNT, PLEN, 3, HEADS, HD)
    positions = jnp.arange(PLEN, dtype=jnp.int32)
    query = jax.vmap(lambda heads_in: rotate(heads_in, positions))(qkv_sum[:, :, 0]).astype(jnp.bfloat16)
    key_rows = jax.vmap(lambda heads_in: rotate(heads_in, positions))(qkv_sum[:, :, 1]).astype(jnp.bfloat16)
    value_rows = qkv_sum[:, :, 2].astype(jnp.bfloat16)
    live_mask = positions[None, :] < prompt_token_length[:, None]
    zero_key = jnp.zeros_like(key_rows)
    key_rows = jnp.where(live_mask[:, :, None, None], key_rows, zero_key)
    value_rows = jnp.where(live_mask[:, :, None, None], value_rows, zero_key)
    pages_new = jnp.stack([key_rows.reshape(PROMPT_COUNT, PLEN, HEADS * HD), value_rows.reshape(PROMPT_COUNT, PLEN, HEADS * HD)], axis=1)
    kv_pages = jnp.zeros_like(pages_new).at[prompt_page_map].set(pages_new)
    scores = jnp.einsum('pqhe,pkhe->phqk', query.astype(jnp.float32), key_rows.astype(jnp.float32), precision=lax.Precision.HIGHEST) / jnp.sqrt(jnp.float32(HD))
    causal = positions[None, :] <= positions[:, None]
    allowed = causal[None, None, :, :] & live_mask[:, None, None, :]
    scores = jnp.where(allowed, scores, jnp.float32(-1e+30))
    top_score = lax.optimization_barrier(jnp.max(scores, axis=-1, keepdims=True))
    expo = jnp.exp(scores - top_score)
    probs = (expo / lax.optimization_barrier(jnp.sum(expo, axis=-1, keepdims=True))).astype(jnp.bfloat16)
    attended = jnp.einsum('phqk,pkhe->pqhe', probs.astype(jnp.float32), value_rows.astype(jnp.float32), precision=lax.Precision.HIGHEST).astype(jnp.bfloat16)
    attended = attended.reshape(TOKENS, HEADS * HD)
    head_width = HEADS * HD // N_ROW
    unit_width = FF // N_ROW
    branch = jnp.zeros((TOKENS, MODEL_WIDTH), jnp.float32)
    for block_index in range(N_ROW):
        low_head = block_index * head_width
        low_unit = block_index * unit_width
        term_row = jnp.dot(attended[:, low_head:low_head + head_width], output_projection[low_head:low_head + head_width], preferred_element_type=jnp.float32)
        term_row = term_row + jnp.dot(hidden[:, low_unit:low_unit + unit_width], down_projection[low_unit:low_unit + unit_width], preferred_element_type=jnp.float32)
        branch = branch + rounded(term_row)
    new_hidden = (hidden_f32 + branch).astype(jnp.bfloat16)
    return (new_hidden, kv_pages)
```

```python
import functools

import jax
import jax.numpy as jnp
import numpy as np
from jax import lax
from jax.experimental import pallas as pl
from jax.experimental.pallas import tpu as pltpu
from jax.sharding import PartitionSpec as P

MODEL_WIDTH = 6144
HD = 96
ROT = 24


def normalize(hidden_f32, moments, gain_row, bias_row):
    row_mean = (moments[0] / MODEL_WIDTH)[:, None]
    row_var = (moments[1] / MODEL_WIDTH)[:, None] - row_mean * row_mean
    return ((hidden_f32 - row_mean) * lax.rsqrt(row_var + 1e-05) * gain_row + bias_row).astype(
        jnp.bfloat16
    )


def rotate(heads_in, positions):
    half_rot = ROT // 2
    inv_freq = 10000.0 ** (-jnp.arange(half_rot, dtype=jnp.float32) * 2.0 / ROT)
    angles = positions.astype(jnp.float32)[:, None] * inv_freq[None, :]
    cosine = jnp.cos(angles)[:, None, :]
    sine_part = jnp.sin(angles)[:, None, :]
    front_part = heads_in[..., :half_rot]
    back_part = heads_in[..., half_rot:ROT]
    return jnp.concatenate(
        [
            front_part * cosine - back_part * sine_part,
            back_part * cosine + front_part * sine_part,
            heads_in[..., ROT:],
        ],
        axis=-1,
    )


def per_device(
    layer_input,
    norm_gain_rows,
    norm_bias_rows,
    query_key_value_weight,
    adapter_down_maps,
    adapter_up_maps,
    output_projection,
    up_projection,
    down_projection,
    prompt_token_length,
    adapter_index,
    prompt_page_map,
):
    col_width = layer_input.shape[1]
    hidden_f32 = layer_input.astype(jnp.float32)
    moments = lax.psum(
        (jnp.sum(hidden_f32, axis=-1), jnp.sum(hidden_f32 * hidden_f32, axis=-1)), "col"
    )
    normed_attn = normalize(hidden_f32, moments, norm_gain_rows[0], norm_bias_rows[0])
    normed_mlp = normalize(hidden_f32, moments, norm_gain_rows[1], norm_bias_rows[1])
    normed_attn, normed_mlp = (
        lax.all_gather(normed_attn, "row", axis=0, tiled=True),
        lax.all_gather(normed_mlp, "row", axis=0, tiled=True),
    )
    col_count = lax.axis_size("col")
    prompt_span = normed_attn.shape[0] // col_count
    wide_weight = query_key_value_weight.reshape(col_width, -1)
    query_key_value_width = wide_weight.shape[1]
    adapter_wide_term = adapter_up_maps.reshape(
        adapter_up_maps.shape[0], adapter_up_maps.shape[1], query_key_value_width
    )
    token_blocks = normed_attn.reshape(col_count, prompt_span, col_width)
    prompt = lax.axis_index("col")
    tok_slice = token_blocks.reshape(lax.axis_size("col") * prompt_span, col_width)
    base_term = jnp.dot(tok_slice, wide_weight, preferred_element_type=jnp.float32)
    chosen = [adapter_index[i] for i in range(col_count)]
    select_down = jnp.concatenate([lax.dynamic_slice_in_dim(adapter_down_maps, i, 1, 0) for i in chosen])
    select_up = jnp.concatenate([lax.dynamic_slice_in_dim(adapter_wide_term, i, 1, 0) for i in chosen])
    low_rank = jnp.einsum(
        "pld,prd->plr", token_blocks, select_down, preferred_element_type=jnp.float32
    ).astype(jnp.bfloat16)
    extra_term = jnp.einsum("plr,prk->plk", low_rank, select_up, preferred_element_type=jnp.float32)
    qkv_rows = lax.psum_scatter(
        (
            base_term
            + extra_term.reshape(lax.axis_size("col") * prompt_span, query_key_value_width)
        ).astype(jnp.bfloat16),
        "col",
        scatter_dimension=0,
        tiled=True,
    ).astype(jnp.float32)
    local_heads = query_key_value_width // (3 * HD)
    qkv_rows = qkv_rows.reshape(prompt_span, 3, local_heads, HD)
    positions = jnp.arange(prompt_span, dtype=jnp.int32)
    prompt_len = lax.dynamic_slice_in_dim(prompt_token_length, prompt, 1, 0)[0]
    live_mask = positions < prompt_len
    query = rotate(qkv_rows[:, 0], positions).astype(jnp.bfloat16)
    key_rows = rotate(qkv_rows[:, 1], positions).astype(jnp.bfloat16)
    value_rows = qkv_rows[:, 2].astype(jnp.bfloat16)
    zero_key = jnp.zeros_like(key_rows)
    key_rows = jnp.where(live_mask[:, None, None], key_rows, zero_key)
    value_rows = jnp.where(live_mask[:, None, None], value_rows, zero_key)
    scores = jnp.einsum(
        "qhe,khe->hqk", query, key_rows, preferred_element_type=jnp.float32
    ) / jnp.sqrt(jnp.float32(HD))
    allowed = (positions[None, :] <= positions[:, None]) & live_mask[None, :]
    scores = jnp.where(allowed[None, :, :], scores, jnp.float32(-1e30))
    top_score = jnp.max(scores, axis=-1, keepdims=True)
    expo = jnp.exp(scores - top_score)
    probs = (expo / jnp.sum(expo, axis=-1, keepdims=True)).astype(jnp.bfloat16)
    attended = jnp.einsum(
        "hqk,khe->qhe", probs, value_rows, preferred_element_type=jnp.float32
    ).astype(jnp.bfloat16)
    attended = attended.reshape(prompt_span, local_heads * HD)
    page_local = jnp.stack(
        [key_rows.reshape(prompt_span, -1), value_rows.reshape(prompt_span, -1)], axis=0
    )[None]
    target_hit = (prompt_page_map == prompt).astype(jnp.bfloat16)
    kv_pages = jnp.einsum(
        "p,pslk->slk",
        target_hit,
        lax.all_gather(page_local, "col", axis=0, tiled=True),
        preferred_element_type=jnp.float32,
    )[None].astype(jnp.bfloat16)
    tok_slice = normed_mlp
    up_rows = lax.psum_scatter(
        jnp.dot(tok_slice, up_projection, preferred_element_type=jnp.float32).astype(jnp.bfloat16),
        "col",
        scatter_dimension=0,
        tiled=True,
    ).astype(jnp.float32)
    hidden = jax.nn.gelu(up_rows, approximate=False).astype(jnp.bfloat16)
    attn_whole, hidden_whole = (
        lax.all_gather(attended, "col", axis=0, tiled=True),
        lax.all_gather(hidden, "col", axis=0, tiled=True),
    )
    branch = lax.psum_scatter(
        (
            jnp.dot(attn_whole, output_projection, preferred_element_type=jnp.float32)
            + jnp.dot(hidden_whole, down_projection, preferred_element_type=jnp.float32)
        ).astype(jnp.bfloat16),
        "row",
        scatter_dimension=0,
        tiled=True,
    ).astype(jnp.float32)
    new_hidden = (layer_input.astype(jnp.float32) + branch).astype(jnp.bfloat16)
    return (new_hidden, kv_pages)


MESH = pl.DeviceIdType.MESH
F32 = jnp.float32
BF16 = jnp.bfloat16


def remote(src, dst, send_sem, recv_sem, device):
    return pltpu.make_async_remote_copy(
        src_ref=src,
        dst_ref=dst,
        send_sem=send_sem,
        recv_sem=recv_sem,
        device_id=device,
        device_id_type=MESH,
    )


def fused_kernel(
    R, C, NU, UC, LE,
    x_ref, gain_ref, bias_ref, wq_hbm, ad_hbm, au_hbm, wo_hbm, wu_hbm, wd_hbm,
    cos_ref, sa_ref, sb_ref, hm_ref, len_ref, aidx_ref, pmap_ref,
    out_ref, kv_ref,
    wq, ad, au, wo, wu, wd,
    xg, mom, momr, st, xn0, xn1, xs, low, qp, rx, qs, qkv, att,
    part, inp, pairb, hid, attb, ao, acc, sst, sbuf, cb, rb,
    w_sem, wu_sem, wq_sem, x_send, x_recv, m_send, m_recv, t_send, t_recv, q_send, q_recv,
    p_send, p_recv, h_send, h_recv, a_send, a_recv, s_send, s_recv, b_send, b_recv,
):
    r = lax.axis_index("row")
    c = lax.axis_index("col")
    par = lax.rem(r, 2)
    chip = lax.div(r, 2)
    sib = r + 1 - 2 * par
    TR, D = x_ref.shape
    S = 2 * TR
    W3 = qs.shape[2]
    N = 4 * NU
    T0 = NU // 2
    end = jnp.logical_or(c == 0, c == C - 1)
    middle = jnp.logical_not(end)
    inner = jnp.where(c < C // 2, c + 1, c - 1)
    outer = jnp.where(c == 1, 0, C - 1)
    flip_x = chip + 1 - 2 * lax.rem(chip, 2)
    flip_y = chip + 2 - 4 * lax.div(chip, 2)
    peers = [chip, flip_x, 3 - chip, flip_y]

    def wu_load(u):
        cols = pl.ds(pl.multiple_of(u * UC, UC), UC)
        return pltpu.make_async_copy(wu_hbm.at[:, cols], wu.at[:, cols], wu_sem.at[u])

    def wq_load(j):
        return pltpu.make_async_copy(wq_hbm.at[j], wq.at[j], wq_sem.at[j])

    loads = [
        pltpu.make_async_copy(a, b, w_sem.at[i])
        for i, (a, b) in enumerate([(ad_hbm, ad), (au_hbm, au), (wd_hbm, wd), (wo_hbm, wo)])
    ]
    for i in range(NU):
        wu_load((T0 + i) % NU).start()
    for j in range(3):
        wq_load(j).start()
    for ld in loads:
        ld.start()

    eye = lax.broadcasted_iota(jnp.int32, (TR, 128), 0) == lax.broadcasted_iota(jnp.int32, (TR, 128), 1)
    line = lax.broadcasted_iota(jnp.int32, (8, 128), 0)
    xf = x_ref[...].astype(F32)
    s1 = jnp.sum(xf, axis=1, keepdims=True)
    s2 = jnp.sum(xf * xf, axis=1, keepdims=True)
    r1 = jnp.sum(jnp.where(eye, s1, 0.0), axis=0, keepdims=True)
    r2 = jnp.sum(jnp.where(eye, s2, 0.0), axis=0, keepdims=True)
    mom[...] = jnp.where(line == 0, r1, jnp.where(line == 1, r2, 0.0))
    acc[...] = jnp.zeros_like(acc)

    barrier = pltpu.get_barrier_semaphore()
    for i in range(1, R):
        pl.semaphore_signal(barrier, inc=1, device_id={"row": lax.rem(r + i, R)}, device_id_type=MESH)
    for i in range(1, C):
        for row in (r, sib):
            pl.semaphore_signal(
                barrier, inc=1, device_id={"row": row, "col": lax.rem(c + i, C)}, device_id_type=MESH
            )
    pl.semaphore_wait(barrier, R - 1 + 2 * (C - 1))

    def x_sib(pos):
        buf = x_ref if pos == 0 else xg.at[pos, par]
        return remote(buf, xg.at[pos, par], x_send.at[0, pos], x_recv.at[pos, par], {"row": sib})

    def x_from_sib(pos):
        return remote(x_ref, xg.at[pos, 1 - par], x_send.at[0, pos], x_recv.at[pos, 1 - par], {"row": sib})

    def x_peer(pos):
        return remote(x_ref, xg.at[pos, par], x_send.at[1, pos], x_recv.at[pos, par], {"row": 2 * peers[pos] + par})

    def m_copy(i, q):
        row = r if q == 0 else sib
        return remote(
            mom, momr.at[c, par], m_send.at[i, q], m_recv.at[c, par], {"row": row, "col": lax.rem(c + i, C)}
        )

    def m_from(i, q):
        src = lax.rem(c + i, C)
        p = par if q == 0 else 1 - par
        return remote(mom, momr.at[src, p], m_send.at[i, q], m_recv.at[src, p], {"row": sib})

    mom_pairs = [(i, q) for i in range(C) for q in range(2) if (i, q) != (0, 0)]
    for i, q in mom_pairs:
        m_copy(i, q).start()
    x_sib(0).start()
    for pos in (1, 3, 2):
        x_peer(pos).start()
    xg[0, par] = x_ref[...]
    tot0, tot1 = mom[...], jnp.zeros((8, 128), F32)
    for i, q in mom_pairs:
        m_from(i, q).wait_recv()
        src = lax.rem(c + i, C)
        if q == 0:
            tot0 = tot0 + momr[src, par]
        else:
            tot1 = tot1 + momr[src, 1 - par]
    st[0, par] = tot0
    st[0, 1 - par] = tot1

    def t_copy(pos, q):
        row = 2 * peers[pos] + (par if q == 0 else 1 - par)
        return remote(st.at[0, par], st.at[pos, par], t_send.at[pos, q], t_recv.at[pos, par], {"row": row})

    for pos in range(1, 4):
        for q in range(2):
            t_copy(pos, q).start()

    def norm(pos):
        for q in range(2):
            tile = st[pos, q]
            mean = jnp.sum(jnp.where(eye, tile[0:1, :], 0.0), axis=1, keepdims=True) / MODEL_WIDTH
            square = jnp.sum(jnp.where(eye, tile[1:2, :], 0.0), axis=1, keepdims=True) / MODEL_WIDTH
            z = (xg[pos, q].astype(F32) - mean) * lax.rsqrt(square - mean * mean + 1e-05)
            xn0[peers[pos], pl.ds(q * TR, TR), :] = (z * gain_ref[0:1, :] + bias_ref[0:1, :]).astype(BF16)
            xn1[pl.ds(pos * S + q * TR, TR), :] = (z * gain_ref[1:2, :] + bias_ref[1:2, :]).astype(BF16)

    x_from_sib(0).wait_recv()
    norm(0)

    inv = []
    for s in range(C):
        v = jnp.int32(0)
        for p in range(1, C):
            v = jnp.where(pmap_ref[p] == s, p, v)
        inv.append(v)
    mine = jnp.int32(0)
    for p in range(1, C):
        mine = jnp.where(pmap_ref[p] == c, p, mine)
    length = len_ref[mine]

    def up(u, lo, rows):
        cols = pl.ds(pl.multiple_of(u * UC, UC), UC)
        return jnp.dot(xn1[lo:lo + rows, :], wu[:, cols], preferred_element_type=F32).astype(BF16)

    def p_copy(k):
        return remote(part.at[k], inp.at[k], p_send.at[k], p_recv.at[k], {"col": inner})

    def pair_copy(k):
        return remote(part.at[k], pairb.at[k], p_send.at[k], h_recv.at[k], {"col": inner})

    def h_copy(k):
        return remote(hid.at[k], hid.at[k], h_send.at[k], h_recv.at[k], {"col": outer})

    def q_copy(dest, j, slot, kk, send, device):
        return remote(qp.at[dest, j], rx.at[slot, kk, j], q_send.at[send, j], q_recv.at[slot, kk, j], {"col": device})

    def q_wait(slot, kk, j):
        remote(qp.at[0, j], rx.at[slot, kk, j], q_send.at[0, j], q_recv.at[slot, kk, j], {"col": inner}).wait_recv()

    def a_copy(s, send, device):
        return remote(attb.at[s], attb.at[s], a_send.at[send], a_recv.at[s], {"col": device})

    def a_wait(s):
        a_copy(s, 0, inner).wait_recv()

    def s_copy(pos):
        return remote(sst.at[pos], sbuf.at[pos], s_send.at[pos], s_recv.at[pos], {"row": sib})

    def b_copy(pos):
        return remote(cb.at[pos], rb.at[pos], b_send.at[pos], b_recv.at[pos], {"row": 2 * peers[pos] + par})

    def half(pos, q):
        return acc[pl.ds(pl.multiple_of(pos * S + q * TR, TR), TR), :]

    def rs_a(pos):
        sst[pos] = half(pos, 1 - par).astype(BF16)
        s_copy(pos).start()

    def rs_b(pos):
        s_copy(pos).wait_recv()
        cb[pos] = (half(pos, par) + sbuf[pos].astype(F32)).astype(BF16)
        b_copy(pos).start()

    def rot(v):
        return (
            v * cos_ref[...]
            + pltpu.roll(v, W3 - ROT // 2, 1) * sa_ref[...]
            + pltpu.roll(v, ROT // 2, 1) * sb_ref[...]
        )

    heads = W3 // HD // 4

    def attention(a):
        @pl.when(a == 0)
        def _():
            @pl.when(end)
            def _():
                for j in range(3):
                    q_wait(1, 0, j)
                    qs[j] = qp[c, j].astype(F32) + rx[1, 0, j].astype(F32)

            live = lax.broadcasted_iota(jnp.int32, (S, W3), 0) < length
            key = jnp.where(live, rot(qs[1]), 0.0).astype(BF16)
            value = jnp.where(live, qs[2], 0.0).astype(BF16)
            qkv[0] = rot(qs[0]).astype(BF16)
            qkv[1] = key
            qkv[2] = value
            kv_ref[0, 0] = key
            kv_ref[0, 1] = value
            att[...] = jnp.zeros_like(att)

        qi = lax.broadcasted_iota(jnp.int32, (S, S), 0)
        ki = lax.broadcasted_iota(jnp.int32, (S, S), 1)
        allowed = jnp.logical_and(ki <= qi, ki < length)
        total = att[...]
        for h in range(heads):
            mask = hm_ref[pl.ds(a * heads + h, 1), :]
            scores = lax.dot_general(
                qkv[0] * mask.astype(BF16), qkv[1], (((1,), (1,)), ((), ())), preferred_element_type=F32
            ) / np.float32(np.sqrt(np.float32(HD)))
            scores = jnp.where(allowed, scores, -1e30)
            expo = jnp.exp(scores - jnp.max(scores, axis=1, keepdims=True))
            probs = (expo / jnp.sum(expo, axis=1, keepdims=True)).astype(BF16)
            total = total + jnp.dot(probs, qkv[2], preferred_element_type=F32) * mask
        att[...] = total

        @pl.when(a == 3)
        def _():
            attb[c] = att[...].astype(BF16)
            a_copy(c, 0, inner).start()

            @pl.when(middle)
            def _():
                a_copy(c, 1, outer).start()

    first_att = jnp.where(end, T0 + 6, T0 + 5)
    WO = 2 * NU + T0 - 1

    def step(v, carry):
        @pl.when(v == T0)
        def _():
            for pos in range(1, 4):
                x_from_sib(pos).wait_recv()
                for q in range(2):
                    remote(st.at[0, q], st.at[pos, q], t_send.at[pos, q], t_recv.at[pos, q], {"row": sib}).wait_recv()
                norm(pos)

        @pl.when(v < T0)
        def _():
            wu_load(v + T0).wait()
            part[v] = up(v + T0, 0, S)

        @pl.when(jnp.logical_and(v >= T0, v < T0 + NU))
        def _():
            u = v - T0

            @pl.when(u < T0)
            def _():
                wu_load(u).wait()

            terms = up(u, S, 3 * S)
            for b in range(3):
                part[T0 + b * NU + u] = terms[b * S:(b + 1) * S]

        @pl.when(jnp.logical_and(v >= T0 + NU, v < 2 * NU))
        def _():
            u = v - T0 - NU
            part[N - T0 + u] = up(u, 0, S)

        @pl.when(jnp.logical_and(end, v < N))
        def _():
            p_copy(v).start()

        @pl.when(v == T0 - 1)
        def _():
            for pos in (1, 3, 2):
                x_peer(pos).wait_recv()
                x_sib(pos).start()

        @pl.when(jnp.logical_and(middle, v < N))
        def _():
            p_copy(v).wait_recv()
            part[v] = (part[v].astype(F32) + inp[v].astype(F32)).astype(BF16)
            pair_copy(v).start()

        @pl.when(v == T0)
        def _():
            for s in range(C):
                xs[pl.ds(s * S, S), :] = xn0[inv[s]]
            loads[0].wait()
            loads[1].wait()
            for s in range(C):
                low[s] = lax.dot_general(
                    xs[pl.ds(s * S, S), :], ad[aidx_ref[inv[s]]], (((1,), (1,)), ((), ())),
                    preferred_element_type=F32,
                ).astype(BF16)

        @pl.when(jnp.logical_and(v >= T0, v < T0 + 3))
        def _():
            j = v - T0
            wq_load(j).wait()
            base = jnp.dot(xs[...], wq[j], preferred_element_type=F32)
            for s in range(C):
                extra = jnp.dot(low[s], au[aidx_ref[inv[s]], j], preferred_element_type=F32)
                qp[s, j] = (base[s * S:(s + 1) * S] + extra).astype(BF16)

        for kk in range(3):
            dest = jnp.where(c < C // 2, C - 1 - kk, kk)

            @pl.when(jnp.logical_and(end, v == T0 + 2 + kk))
            def _():
                for j in range(3):
                    q_copy(dest, j, 0, kk, kk, inner).start()

            @pl.when(jnp.logical_and(middle, v == T0 + 2 + kk))
            def _():
                for j in range(3):
                    if kk == 1:
                        q_wait(1, 0, j)
                        qp[outer, j] = (qp[outer, j].astype(F32) + rx[1, 0, j].astype(F32)).astype(BF16)
                        q_copy(outer, j, 1, 0, 2, outer).start()
                    q_wait(0, kk, j)
                    if kk < 2:
                        qp[dest, j] = (qp[dest, j].astype(F32) + rx[0, kk, j].astype(F32)).astype(BF16)
                        q_copy(dest, j, 1, kk, kk, inner).start()
                    else:
                        q_wait(1, 1, j)
                        qs[j] = qp[c, j].astype(F32) + rx[0, 2, j].astype(F32) + rx[1, 1, j].astype(F32)

        k = jnp.where(end, v - LE, v - 2)

        @pl.when(k == 0)
        def _():
            loads[2].wait()

        @pl.when(jnp.logical_and(k >= 0, k < N))
        def _():
            @pl.when(middle)
            def _():
                pair_copy(k).wait_recv()
                u = part[k].astype(F32) + pairb[k].astype(F32)
                hid[k] = (0.5 * u * (1.0 + lax.erf(u * np.float32(np.sqrt(0.5))))).astype(BF16)
                h_copy(k).start()

            @pl.when(end)
            def _():
                h_copy(k).wait_recv()

            tau = k + T0
            pos = lax.rem(lax.div(tau, NU), 4)
            u0 = lax.rem(tau, NU)
            rows = pl.ds(pl.multiple_of(pos * S, S), S)
            units = pl.ds(pl.multiple_of(u0 * UC, UC), UC)
            acc[rows, :] += jnp.dot(hid[k], wd[units, :], preferred_element_type=F32)

        a = v - first_att

        @pl.when(jnp.logical_and(a >= 0, a < 4))
        def _():
            attention(a)

        @pl.when(jnp.logical_and(middle, v == T0 + 10))
        def _():
            a_wait(outer)
            a_copy(outer, 2, inner).start()
            a_wait(inner)
            a_copy(inner, 3, outer).start()

        @pl.when(jnp.logical_and(middle, v == T0 + 12))
        def _():
            a_wait(C - 1 - outer)
            a_copy(C - 1 - outer, 4, outer).start()

        @pl.when(k == WO)
        def _():
            @pl.when(end)
            def _():
                a_wait(inner)
                a_wait(C - 1 - inner)
                a_wait(C - 1 - c)

            loads[3].wait()
            for pos in range(4):
                ao[pl.ds(pos * S, S), :] = attb[pmap_ref[peers[pos]]]
            acc[...] += jnp.dot(ao[...], wo[...], preferred_element_type=F32)

        @pl.when(k == WO + 1)
        def _():
            rs_a(1)

        @pl.when(k == WO + 2)
        def _():
            rs_b(1)
            rs_a(2)

        @pl.when(k == WO + 3)
        def _():
            rs_b(2)

        @pl.when(k == N - T0 - 1)
        def _():
            rs_a(3)

        @pl.when(k == N - T0)
        def _():
            rs_b(3)

        return carry

    lax.fori_loop(0, N + LE, step, 0)

    rs_a(0)
    total = x_ref[...].astype(F32) + half(0, par)
    for pos in (1, 2, 3):
        b_copy(pos).wait_recv()
        total = total + rb[pos].astype(F32)
    s_copy(0).wait_recv()
    out_ref[...] = (total + sbuf[0].astype(F32)).astype(BF16)

    for pos in range(4):
        x_sib(pos).wait_send()
        s_copy(pos).wait_send()
    for pos in range(1, 4):
        x_peer(pos).wait_send()
        b_copy(pos).wait_send()
        for q in range(2):
            t_copy(pos, q).wait_send()
    for i, q in mom_pairs:
        m_copy(i, q).wait_send()
    for kk in range(3):
        for j in range(3):
            q_copy(0, j, 0, 0, kk, inner).wait_send()
    a_copy(0, 0, inner).wait_send()

    @pl.when(middle)
    def _():
        for i in range(1, 5):
            a_copy(0, i, inner).wait_send()

    def drain(k, carry):
        p_copy(k).wait_send()

        @pl.when(middle)
        def _():
            h_copy(k).wait_send()

        return carry

    lax.fori_loop(0, N, drain, 0)


def rotary_tables(span, width):
    half = ROT // 2
    inv_freq = np.float32(10000.0) ** (-np.arange(half, dtype=np.float32) * np.float32(2.0) / np.float32(ROT))
    angles = np.arange(span, dtype=np.float32)[:, None] * inv_freq[None, :].astype(np.float32)
    cosine, sine = np.cos(angles), np.sin(angles)
    cos = np.ones((span, width), np.float32)
    front = np.zeros((span, width), np.float32)
    back = np.zeros((span, width), np.float32)
    for low in range(0, width, HD):
        cos[:, low:low + half] = cosine
        cos[:, low + half:low + ROT] = cosine
        front[:, low:low + half] = -sine
        back[:, low + half:low + ROT] = sine
    heads = (np.arange(width)[None, :] // HD == np.arange(width // HD)[:, None]).astype(np.float32)
    return cos, front, back, heads


def fused(
    layer_input, norm_gain_rows, norm_bias_rows, query_key_value_weight, adapter_down_maps,
    adapter_up_maps, output_projection, up_projection, down_projection, prompt_token_length,
    adapter_index, prompt_page_map,
):
    R, C = lax.axis_size("row"), lax.axis_size("col")
    TR, D = layer_input.shape
    T = TR * R
    S = T // C
    W3 = query_key_value_weight.shape[2]
    U = up_projection.shape[1]
    UC = 512
    NU = U // UC
    N = 4 * NU
    wq = jnp.transpose(query_key_value_weight, (1, 0, 2))
    au = jnp.transpose(adapter_up_maps, (0, 2, 1, 3))
    tables = [jnp.asarray(t) for t in rotary_tables(S, W3)]
    vm = pl.BlockSpec(memory_space=pltpu.VMEM)
    sm = pl.BlockSpec(memory_space=pltpu.SMEM)
    hbm = pl.BlockSpec(memory_space=pl.ANY)
    dma = pltpu.SemaphoreType.DMA
    V = pltpu.VMEM
    return pl.pallas_call(
        functools.partial(fused_kernel, R, C, NU, UC, 10),
        out_shape=(
            jax.ShapeDtypeStruct((TR, D), BF16),
            jax.ShapeDtypeStruct((1, 2, S, W3), BF16),
        ),
        in_specs=[vm] * 3 + [hbm] * 6 + [vm] * 4 + [sm] * 3,
        out_specs=(vm, vm),
        scratch_shapes=[
            V(wq.shape, BF16), V(adapter_down_maps.shape, BF16), V(au.shape, BF16),
            V(output_projection.shape, BF16), V(up_projection.shape, BF16), V(down_projection.shape, BF16),
            V((4, 2, TR, D), BF16), V((8, 128), F32), V((C, 2, 8, 128), F32), V((4, 2, 8, 128), F32),
            V((C, S, D), BF16), V((T, D), BF16), V((T, D), BF16), V((C, S, au.shape[2]), BF16),
            V((C, 3, S, W3), BF16), V((2, 3, 3, S, W3), BF16), V((3, S, W3), F32), V((3, S, W3), BF16), V((S, W3), F32),
            V((N, S, UC), BF16), V((N, S, UC), BF16), V((N, S, UC), BF16), V((N, S, UC), BF16),
            V((C, S, W3), BF16), V((T, W3), BF16), V((T, D), F32),
            V((4, TR, D), BF16), V((4, TR, D), BF16), V((4, TR, D), BF16), V((4, TR, D), BF16),
            dma((4,)), dma((NU,)), dma((3,)), dma((2, 4)), dma((4, 2)), dma((C, 2)), dma((C, 2)), dma((4, 2)), dma((4, 2)),
            dma((3, 3)), dma((2, 3, 3)), dma((N,)), dma((N,)), dma((N,)), dma((N,)),
            dma((5,)), dma((C,)), dma((4,)), dma((4,)), dma((4,)), dma((4,)),
        ],
        compiler_params=pltpu.CompilerParams(
            collective_id=0, has_side_effects=True, vmem_limit_bytes=63 * 1024 * 1024
        ),
    )(
        layer_input, norm_gain_rows, norm_bias_rows, wq, adapter_down_maps, au,
        output_projection, up_projection, down_projection, *tables,
        prompt_token_length, adapter_index, prompt_page_map,
    )


def layer(*args):
    rows, weight, up = args[0].shape[0], args[3], args[7]
    R, C = lax.axis_size("row"), lax.axis_size("col")
    span = rows * R // C
    fits = R == 8 and C == 4 and span == 2 * rows and rows % 16 == 0 and rows <= 128
    fits = fits and weight.shape[2] % 128 == 0 and weight.shape[0] % 128 == 0 and up.shape[1] == 6 * 512
    fits = fits and weight.shape[2] % (4 * HD) == 0
    return fused(*args) if fits else per_device(*args)


def solution(mesh):
    return jax.shard_map(
        layer,
        mesh=mesh,
        in_specs=(
            P("row", "col"),
            P(None, "col"),
            P(None, "col"),
            P("col", None, "row"),
            P(None, None, "col"),
            P(None, None, None, "row"),
            P("row", "col"),
            P("col", "row"),
            P("row", "col"),
            P(),
            P(),
            P(),
        ),
        out_specs=(P("row", "col"), P("col", None, None, "row")),
        check_vma=False,
    )
```

```python
import functools

import jax
import jax.numpy as jnp
import numpy as np
from jax import lax
from jax.experimental import pallas as pl
from jax.experimental.pallas import tpu as pltpu
from jax.sharding import PartitionSpec as P

MODEL_WIDTH = 6144
HD = 96
ROT = 24


def normalize(hidden_f32, moments, gain_row, bias_row):
    row_mean = (moments[0] / MODEL_WIDTH)[:, None]
    row_var = (moments[1] / MODEL_WIDTH)[:, None] - row_mean * row_mean
    return ((hidden_f32 - row_mean) * lax.rsqrt(row_var + 1e-05) * gain_row + bias_row).astype(
        jnp.bfloat16
    )


def rotate(heads_in, positions):
    half_rot = ROT // 2
    inv_freq = 10000.0 ** (-jnp.arange(half_rot, dtype=jnp.float32) * 2.0 / ROT)
    angles = positions.astype(jnp.float32)[:, None] * inv_freq[None, :]
    cosine = jnp.cos(angles)[:, None, :]
    sine_part = jnp.sin(angles)[:, None, :]
    front_part = heads_in[..., :half_rot]
    back_part = heads_in[..., half_rot:ROT]
    return jnp.concatenate(
        [
            front_part * cosine - back_part * sine_part,
            back_part * cosine + front_part * sine_part,
            heads_in[..., ROT:],
        ],
        axis=-1,
    )


def per_device(
    layer_input,
    norm_gain_rows,
    norm_bias_rows,
    query_key_value_weight,
    adapter_down_maps,
    adapter_up_maps,
    output_projection,
    up_projection,
    down_projection,
    prompt_token_length,
    adapter_index,
    prompt_page_map,
):
    col_width = layer_input.shape[1]
    hidden_f32 = layer_input.astype(jnp.float32)
    moments = lax.psum(
        (jnp.sum(hidden_f32, axis=-1), jnp.sum(hidden_f32 * hidden_f32, axis=-1)), "col"
    )
    normed_attn = normalize(hidden_f32, moments, norm_gain_rows[0], norm_bias_rows[0])
    normed_mlp = normalize(hidden_f32, moments, norm_gain_rows[1], norm_bias_rows[1])
    normed_attn, normed_mlp = (
        lax.all_gather(normed_attn, "row", axis=0, tiled=True),
        lax.all_gather(normed_mlp, "row", axis=0, tiled=True),
    )
    col_count = lax.axis_size("col")
    prompt_span = normed_attn.shape[0] // col_count
    wide_weight = query_key_value_weight.reshape(col_width, -1)
    query_key_value_width = wide_weight.shape[1]
    adapter_wide_term = adapter_up_maps.reshape(
        adapter_up_maps.shape[0], adapter_up_maps.shape[1], query_key_value_width
    )
    token_blocks = normed_attn.reshape(col_count, prompt_span, col_width)
    prompt = lax.axis_index("col")
    tok_slice = token_blocks.reshape(lax.axis_size("col") * prompt_span, col_width)
    base_term = jnp.dot(tok_slice, wide_weight, preferred_element_type=jnp.float32)
    chosen = [adapter_index[i] for i in range(col_count)]
    select_down = jnp.concatenate([lax.dynamic_slice_in_dim(adapter_down_maps, i, 1, 0) for i in chosen])
    select_up = jnp.concatenate([lax.dynamic_slice_in_dim(adapter_wide_term, i, 1, 0) for i in chosen])
    low_rank = jnp.einsum(
        "pld,prd->plr", token_blocks, select_down, preferred_element_type=jnp.float32
    ).astype(jnp.bfloat16)
    extra_term = jnp.einsum("plr,prk->plk", low_rank, select_up, preferred_element_type=jnp.float32)
    qkv_rows = lax.psum_scatter(
        (
            base_term
            + extra_term.reshape(lax.axis_size("col") * prompt_span, query_key_value_width)
        ).astype(jnp.bfloat16),
        "col",
        scatter_dimension=0,
        tiled=True,
    ).astype(jnp.float32)
    local_heads = query_key_value_width // (3 * HD)
    qkv_rows = qkv_rows.reshape(prompt_span, 3, local_heads, HD)
    positions = jnp.arange(prompt_span, dtype=jnp.int32)
    prompt_len = lax.dynamic_slice_in_dim(prompt_token_length, prompt, 1, 0)[0]
    live_mask = positions < prompt_len
    query = rotate(qkv_rows[:, 0], positions).astype(jnp.bfloat16)
    key_rows = rotate(qkv_rows[:, 1], positions).astype(jnp.bfloat16)
    value_rows = qkv_rows[:, 2].astype(jnp.bfloat16)
    zero_key = jnp.zeros_like(key_rows)
    key_rows = jnp.where(live_mask[:, None, None], key_rows, zero_key)
    value_rows = jnp.where(live_mask[:, None, None], value_rows, zero_key)
    scores = jnp.einsum(
        "qhe,khe->hqk", query, key_rows, preferred_element_type=jnp.float32
    ) / jnp.sqrt(jnp.float32(HD))
    allowed = (positions[None, :] <= positions[:, None]) & live_mask[None, :]
    scores = jnp.where(allowed[None, :, :], scores, jnp.float32(-1e30))
    top_score = jnp.max(scores, axis=-1, keepdims=True)
    expo = jnp.exp(scores - top_score)
    probs = (expo / jnp.sum(expo, axis=-1, keepdims=True)).astype(jnp.bfloat16)
    attended = jnp.einsum(
        "hqk,khe->qhe", probs, value_rows, preferred_element_type=jnp.float32
    ).astype(jnp.bfloat16)
    attended = attended.reshape(prompt_span, local_heads * HD)
    page_local = jnp.stack(
        [key_rows.reshape(prompt_span, -1), value_rows.reshape(prompt_span, -1)], axis=0
    )[None]
    target_hit = (prompt_page_map == prompt).astype(jnp.bfloat16)
    kv_pages = jnp.einsum(
        "p,pslk->slk",
        target_hit,
        lax.all_gather(page_local, "col", axis=0, tiled=True),
        preferred_element_type=jnp.float32,
    )[None].astype(jnp.bfloat16)
    tok_slice = normed_mlp
    up_rows = lax.psum_scatter(
        jnp.dot(tok_slice, up_projection, preferred_element_type=jnp.float32).astype(jnp.bfloat16),
        "col",
        scatter_dimension=0,
        tiled=True,
    ).astype(jnp.float32)
    hidden = jax.nn.gelu(up_rows, approximate=False).astype(jnp.bfloat16)
    attn_whole, hidden_whole = (
        lax.all_gather(attended, "col", axis=0, tiled=True),
        lax.all_gather(hidden, "col", axis=0, tiled=True),
    )
    branch = lax.psum_scatter(
        (
            jnp.dot(attn_whole, output_projection, preferred_element_type=jnp.float32)
            + jnp.dot(hidden_whole, down_projection, preferred_element_type=jnp.float32)
        ).astype(jnp.bfloat16),
        "row",
        scatter_dimension=0,
        tiled=True,
    ).astype(jnp.float32)
    new_hidden = (layer_input.astype(jnp.float32) + branch).astype(jnp.bfloat16)
    return (new_hidden, kv_pages)


MESH = pl.DeviceIdType.MESH
F32 = jnp.float32
BF16 = jnp.bfloat16


def remote(src, dst, send_sem, recv_sem, device):
    return pltpu.make_async_remote_copy(
        src_ref=src,
        dst_ref=dst,
        send_sem=send_sem,
        recv_sem=recv_sem,
        device_id=device,
        device_id_type=MESH,
    )


def fused_kernel(
    R, C, NU, UC, LE, SUB,
    x_hbm, gain_hbm, bias_hbm, wq_hbm, ad_hbm, au_hbm, wo_hbm, wu_hbm, wd_hbm,
    tab_hbm, hm_hbm, len_ref, aidx_ref, pmap_ref,
    out_ref, kv_hbm,
    x_ref, gain_ref, bias_ref, tab, hm_ref, wq, ad, au, wo, wu, wd,
    xg, mom, momr, st, xn0, xn1, xs, low, qp, rx, qs, qkv, att, kvb,
    part, inp, pairb, hid, attb, ao, acc, sst, sbuf, cb, rb,
    in_sem, kv_sem, w_sem, wu_sem, wq_sem, x_send, x_recv, m_send, m_recv, t_send, t_recv, q_send, q_recv,
    p_send, p_recv, h_send, h_recv, a_send, a_recv, s_send, s_recv, b_send, b_recv,
):
    r = lax.axis_index("row")
    c = lax.axis_index("col")
    par = lax.rem(r, 2)
    chip = lax.div(r, 2)
    sib = r + 1 - 2 * par
    TR, D = x_ref.shape
    S = 2 * TR
    HW = att.shape[1]
    W3 = 2 * HW
    UQ = UC // SUB
    N = 4 * NU
    T0 = NU // 2
    end = jnp.logical_or(c == 0, c == C - 1)
    middle = jnp.logical_not(end)
    inner = jnp.where(c < C // 2, c + 1, c - 1)
    outer = jnp.where(c == 1, 0, C - 1)
    flip_x = chip + 1 - 2 * lax.rem(chip, 2)
    flip_y = chip + 2 - 4 * lax.div(chip, 2)
    peers = [chip, flip_x, 3 - chip, flip_y]

    def wu_load(u):
        cols = pl.ds(pl.multiple_of(u * UC, UC), UC)
        return pltpu.make_async_copy(wu_hbm.at[:, cols], wu.at[:, cols], wu_sem.at[u])

    def wq_load(j):
        return pltpu.make_async_copy(wq_hbm.at[j], wq.at[j], wq_sem.at[j])

    loads = [
        pltpu.make_async_copy(a, b, w_sem.at[i])
        for i, (a, b) in enumerate([(ad_hbm, ad), (au_hbm, au), (wd_hbm, wd), (wo_hbm, wo)])
    ]
    early = [
        pltpu.make_async_copy(a, b, in_sem.at[i])
        for i, (a, b) in enumerate([(x_hbm, x_ref), (gain_hbm, gain_ref), (bias_hbm, bias_ref), (tab_hbm, tab), (hm_hbm, hm_ref)])
    ]
    for i in range(3):
        early[i].start()
    barrier = pltpu.get_barrier_semaphore()
    for i in range(1, R):
        pl.semaphore_signal(barrier, inc=1, device_id={"row": lax.rem(r + i, R)}, device_id_type=MESH)
    for i in range(1, C):
        for row in (r, sib):
            pl.semaphore_signal(
                barrier, inc=1, device_id={"row": row, "col": lax.rem(c + i, C)}, device_id_type=MESH
            )
    for i in range(NU):
        wu_load((T0 + i) % NU).start()
    for j in range(3):
        wq_load(j).start()
    for ld in loads[:2] + early[3:] + loads[2:]:
        ld.start()
    acc[...] = jnp.zeros_like(acc)
    early[0].wait()

    eye = lax.broadcasted_iota(jnp.int32, (TR, 128), 0) == lax.broadcasted_iota(jnp.int32, (TR, 128), 1)
    line = lax.broadcasted_iota(jnp.int32, (8, 128), 0)
    xf = x_ref[...].astype(F32)
    s1 = jnp.sum(xf, axis=1, keepdims=True)
    s2 = jnp.sum(xf * xf, axis=1, keepdims=True)
    r1 = jnp.sum(jnp.where(eye, s1, 0.0), axis=0, keepdims=True)
    r2 = jnp.sum(jnp.where(eye, s2, 0.0), axis=0, keepdims=True)
    mom[...] = jnp.where(line == 0, r1, jnp.where(line == 1, r2, 0.0))

    pl.semaphore_wait(barrier, R - 1 + 2 * (C - 1))

    def x_sib(pos):
        buf = x_ref if pos == 0 else xg.at[pos, par]
        return remote(buf, xg.at[pos, par], x_send.at[0, pos], x_recv.at[pos, par], {"row": sib})

    def x_from_sib(pos):
        return remote(x_ref, xg.at[pos, 1 - par], x_send.at[0, pos], x_recv.at[pos, 1 - par], {"row": sib})

    def x_peer(pos):
        return remote(x_ref, xg.at[pos, par], x_send.at[1, pos], x_recv.at[pos, par], {"row": 2 * peers[pos] + par})

    def m_copy(i, q):
        row = r if q == 0 else sib
        return remote(
            mom, momr.at[c, par], m_send.at[i, q], m_recv.at[c, par], {"row": row, "col": lax.rem(c + i, C)}
        )

    def m_from(i, q):
        src = lax.rem(c + i, C)
        p = par if q == 0 else 1 - par
        return remote(mom, momr.at[src, p], m_send.at[i, q], m_recv.at[src, p], {"row": sib})

    mom_pairs = [(i, q) for i in range(C) for q in range(2) if (i, q) != (0, 0)]
    for i, q in mom_pairs:
        m_copy(i, q).start()
    x_sib(0).start()
    for pos in (1, 3, 2):
        x_peer(pos).start()
    xg[0, par] = x_ref[...]
    tot0, tot1 = mom[...], jnp.zeros((8, 128), F32)
    for i, q in mom_pairs:
        m_from(i, q).wait_recv()
        src = lax.rem(c + i, C)
        if q == 0:
            tot0 = tot0 + momr[src, par]
        else:
            tot1 = tot1 + momr[src, 1 - par]
    st[0, par] = tot0
    st[0, 1 - par] = tot1

    def t_copy(pos, q):
        row = 2 * peers[pos] + (par if q == 0 else 1 - par)
        return remote(st.at[0, par], st.at[pos, par], t_send.at[pos, q], t_recv.at[pos, par], {"row": row})

    def norm(pos, mlp):
        for q in range(2):
            tile = st[pos, q]
            mean = jnp.sum(jnp.where(eye, tile[0:1, :], 0.0), axis=1, keepdims=True) / MODEL_WIDTH
            square = jnp.sum(jnp.where(eye, tile[1:2, :], 0.0), axis=1, keepdims=True) / MODEL_WIDTH
            z = (xg[pos, q].astype(F32) - mean) * lax.rsqrt(square - mean * mean + 1e-05)
            if mlp:
                xn1[pl.ds(pos * S + q * TR, TR), :] = (z * gain_ref[1:2, :] + bias_ref[1:2, :]).astype(BF16)
            else:
                xn0[peers[pos], pl.ds(q * TR, TR), :] = (z * gain_ref[0:1, :] + bias_ref[0:1, :]).astype(BF16)

    early[1].wait()
    early[2].wait()
    x_from_sib(0).wait_recv()
    norm(0, True)

    inv = []
    for s in range(C):
        v = jnp.int32(0)
        for p in range(1, C):
            v = jnp.where(pmap_ref[p] == s, p, v)
        inv.append(v)
    mine = jnp.int32(0)
    for p in range(1, C):
        mine = jnp.where(pmap_ref[p] == c, p, mine)
    length = len_ref[mine]

    def up(u, lo, rows):
        cols = pl.ds(pl.multiple_of(u * UC, UC), UC)
        return jnp.dot(xn1[lo:lo + rows, :], wu[:, cols], preferred_element_type=F32).astype(BF16)

    def p_copy(k):
        return remote(part.at[k], inp.at[k], p_send.at[k], p_recv.at[k], {"col": inner})

    def pair_copy(k):
        return remote(part.at[k], pairb.at[k], p_send.at[k], h_recv.at[k], {"col": inner})

    def h_copy(k):
        return remote(hid.at[k], hid.at[k], h_send.at[k], h_recv.at[k], {"col": outer})

    def last(buf, i):
        return buf.at[N - 1, :, pl.ds(i * UQ, UQ)]

    def p_last(i):
        return remote(last(part, i), last(inp, i), p_send.at[N - 1 + i], p_recv.at[N - 1 + i], {"col": inner})

    def pair_last(i):
        return remote(last(part, i), last(pairb, i), p_send.at[N - 1 + i], h_recv.at[N - 1 + i], {"col": inner})

    def h_last(i):
        return remote(last(hid, i), last(hid, i), h_send.at[N - 1 + i], h_recv.at[N - 1 + i], {"col": outer})

    def q_copy(dest, half, slot, kk, send, device):
        return remote(
            qp.at[dest, half], rx.at[slot, kk, half], q_send.at[send, half], q_recv.at[slot, kk, half], {"col": device}
        )

    def q_wait(slot, kk, half):
        q_copy(0, half, slot, kk, 0, inner).wait_recv()

    def a_copy(s, half, send, device):
        return remote(attb.at[s, half], attb.at[s, half], a_send.at[send, half], a_recv.at[s, half], {"col": device})

    def a_wait(s, half):
        a_copy(s, half, 0, inner).wait_recv()

    def kv_copy(half):
        cols = pl.ds(half * HW, HW)
        return pltpu.make_async_copy(kvb.at[half], kv_hbm.at[0, :, :, cols], kv_sem.at[half])

    def gelu(u):
        return (0.5 * u * (1.0 + lax.erf(u * np.float32(np.sqrt(0.5))))).astype(BF16)

    def s_copy(pos):
        return remote(sst.at[pos], sbuf.at[pos], s_send.at[pos], s_recv.at[pos], {"row": sib})

    def b_copy(pos):
        return remote(cb.at[pos], rb.at[pos], b_send.at[pos], b_recv.at[pos], {"row": 2 * peers[pos] + par})

    def rows_of(pos, q):
        return acc[pl.ds(pl.multiple_of(pos * S + q * TR, TR), TR), :]

    def rs_a(pos):
        sst[pos] = rows_of(pos, 1 - par).astype(BF16)
        s_copy(pos).start()

    def rs_b(pos):
        s_copy(pos).wait_recv()
        cb[pos] = (rows_of(pos, par) + sbuf[pos].astype(F32)).astype(BF16)
        b_copy(pos).start()

    def rot(v):
        return (
            v * tab[0]
            + pltpu.roll(v, HW - ROT // 2, 1) * tab[1]
            + pltpu.roll(v, ROT // 2, 1) * tab[2]
        )

    heads = HW // HD // 2

    def attention(half, a):
        if a == 0:
            if half == 0:
                early[3].wait()
                early[4].wait()

            @pl.when(end)
            def _():
                q_wait(1, 0, half)
                for j in range(3):
                    qs[j] = qp[c, half, j].astype(F32) + rx[1, 0, half, j].astype(F32)

            live = lax.broadcasted_iota(jnp.int32, (S, HW), 0) < length
            key = jnp.where(live, rot(qs[1]), 0.0).astype(BF16)
            value = jnp.where(live, qs[2], 0.0).astype(BF16)
            qkv[0] = rot(qs[0]).astype(BF16)
            qkv[1] = key
            qkv[2] = value
            kvb[half, 0] = key
            kvb[half, 1] = value
            kv_copy(half).start()

        qi = lax.broadcasted_iota(jnp.int32, (S, S), 0)
        ki = lax.broadcasted_iota(jnp.int32, (S, S), 1)
        allowed = jnp.logical_and(ki <= qi, ki < length)
        total = jnp.zeros((S, HW), F32) if a == 0 else att[...]
        for h in range(heads):
            mask = hm_ref[a * heads + h:a * heads + h + 1, :]
            scores = lax.dot_general(
                qkv[0] * mask.astype(BF16), qkv[1], (((1,), (1,)), ((), ())), preferred_element_type=F32
            ) / np.float32(np.sqrt(np.float32(HD)))
            scores = jnp.where(allowed, scores, -1e30)
            expo = jnp.exp(scores - jnp.max(scores, axis=1, keepdims=True))
            probs = (expo / jnp.sum(expo, axis=1, keepdims=True)).astype(BF16)
            total = total + jnp.dot(probs, qkv[2], preferred_element_type=F32) * mask
        if a == 0:
            att[...] = total
        else:
            attb[c, half] = total.astype(BF16)
            a_copy(c, half, 0, inner).start()

            @pl.when(middle)
            def _():
                a_copy(c, half, 1, outer).start()

    WO = 2 * NU + T0
    att_at = [T0 + 5, jnp.where(end, T0 + 9, T0 + 8)]

    def first_terms(v):
        @pl.when(v == T0)
        def _():
            for pos in range(1, 4):
                x_from_sib(pos).wait_recv()
                for q in range(2):
                    remote(st.at[0, q], st.at[pos, q], t_send.at[pos, q], t_recv.at[pos, q], {"row": sib}).wait_recv()
                norm(pos, True)

        @pl.when(v < T0)
        def _():
            wu_load(v + T0).wait()
            part[v] = up(v + T0, 0, S)

        @pl.when(jnp.logical_and(v >= T0, v < T0 + NU))
        def _():
            u = v - T0

            @pl.when(u < T0)
            def _():
                wu_load(u).wait()

            terms = up(u, S, 3 * S)
            for b in range(3):
                part[T0 + b * NU + u] = terms[b * S:(b + 1) * S]

        @pl.when(v >= T0 + NU)
        def _():
            u = v - T0 - NU
            part[N - T0 + u] = up(u, 0, S)

    def share(v):
        @pl.when(v < N - 1)
        def _():
            @pl.when(end)
            def _():
                p_copy(v).start()

            @pl.when(middle)
            def _():
                p_copy(v).wait_recv()
                part[v] = (part[v].astype(F32) + inp[v].astype(F32)).astype(BF16)
                pair_copy(v).start()

        @pl.when(v == N - 1)
        def _():
            @pl.when(end)
            def _():
                for i in range(SUB):
                    p_last(i).start()

            @pl.when(middle)
            def _():
                for i in range(SUB):
                    p_last(i).wait_recv()
                    cols = slice(i * UQ, (i + 1) * UQ)
                    part[N - 1, :, cols] = (
                        part[N - 1, :, cols].astype(F32) + inp[N - 1, :, cols].astype(F32)
                    ).astype(BF16)
                    pair_last(i).start()

    def qkv_terms(v):
        @pl.when(v == 0)
        def _():
            for pos in range(1, 4):
                for q in range(2):
                    t_copy(pos, q).start()

        @pl.when(v == T0 - 1)
        def _():
            for pos in (1, 3, 2):
                x_peer(pos).wait_recv()
                x_sib(pos).start()

        @pl.when(v == T0)
        def _():
            for pos in range(4):
                norm(pos, False)
            for s in range(C):
                xs[pl.ds(s * S, S), :] = xn0[inv[s]]
            loads[0].wait()
            loads[1].wait()
            for s in range(C):
                low[s] = lax.dot_general(
                    xs[pl.ds(s * S, S), :], ad[aidx_ref[inv[s]]], (((1,), (1,)), ((), ())),
                    preferred_element_type=F32,
                ).astype(BF16)

        @pl.when(v >= T0)
        def _():
            j = v - T0
            wq_load(j).wait()
            base = jnp.dot(xs[...], wq[j], preferred_element_type=F32)
            for s in range(C):
                extra = jnp.dot(low[s], au[aidx_ref[inv[s]], j], preferred_element_type=F32)
                term = (base[s * S:(s + 1) * S] + extra).astype(BF16)
                for half in range(2):
                    qp[s, half, j] = term[:, half * HW:(half + 1) * HW]

    def qkv_share(v):
        for m in range(6):
            half, kk = m // 3, m % 3
            dest = jnp.where(c < C // 2, C - 1 - kk, kk)

            @pl.when(v == T0 + 2 + m)
            def _():
                @pl.when(end)
                def _():
                    q_copy(dest, half, 0, kk, kk, inner).start()

                @pl.when(middle)
                def _():
                    if kk == 1:
                        q_wait(1, 0, half)
                        for j in range(3):
                            qp[outer, half, j] = (
                                qp[outer, half, j].astype(F32) + rx[1, 0, half, j].astype(F32)
                            ).astype(BF16)
                        q_copy(outer, half, 1, 0, 2, outer).start()
                    q_wait(0, kk, half)
                    if kk < 2:
                        for j in range(3):
                            qp[dest, half, j] = (
                                qp[dest, half, j].astype(F32) + rx[0, kk, half, j].astype(F32)
                            ).astype(BF16)
                        q_copy(dest, half, 1, kk, kk, inner).start()
                    else:
                        q_wait(1, 1, half)
                        for j in range(3):
                            qs[j] = (
                                qp[c, half, j].astype(F32) + rx[0, 2, half, j].astype(F32) + rx[1, 1, half, j].astype(F32)
                            )

    def attend(v):
        for half in range(2):
            for a in range(2):
                @pl.when(v == att_at[half] + a)
                def _():
                    attention(half, a)

        @pl.when(middle)
        def _():
            for half, at in enumerate([(T0 + 7, T0 + 8, T0 + 9), (T0 + 11, T0 + 11, T0 + 13)]):
                @pl.when(v == at[0])
                def _():
                    a_wait(outer, half)
                    a_copy(outer, half, 2, inner).start()

                @pl.when(v == at[1])
                def _():
                    a_wait(inner, half)
                    a_copy(inner, half, 3, outer).start()

                @pl.when(v == at[2])
                def _():
                    a_wait(C - 1 - outer, half)
                    a_copy(C - 1 - outer, half, 4, outer).start()

    def late(k):
        @pl.when(k == WO)
        def _():
            @pl.when(end)
            def _():
                for half in range(2):
                    a_wait(inner, half)
                    a_wait(C - 1 - inner, half)
                    a_wait(C - 1 - c, half)

            loads[3].wait()
            for pos in range(4):
                for half in range(2):
                    ao[pl.ds(pos * S, S), pl.ds(half * HW, HW)] = attb[pmap_ref[peers[pos]], half]
            acc[...] += jnp.dot(ao[...], wo[...], preferred_element_type=F32)

        @pl.when(k == WO + 1)
        def _():
            rs_a(1)

        @pl.when(k == WO + 2)
        def _():
            rs_b(1)
            rs_a(2)

        @pl.when(k == WO + 3)
        def _():
            rs_b(2)

        @pl.when(k == N - T0 - 1)
        def _():
            rs_a(3)

        @pl.when(k == N - T0)
        def _():
            rs_b(3)

    def finish(k, carry):
        @pl.when(k == 0)
        def _():
            loads[2].wait()

        @pl.when(k < N - 1)
        def _():
            @pl.when(middle)
            def _():
                pair_copy(k).wait_recv()
                hid[k] = gelu(part[k].astype(F32) + pairb[k].astype(F32))
                h_copy(k).start()

            @pl.when(end)
            def _():
                h_copy(k).wait_recv()

            tau = k + T0
            pos = lax.rem(lax.div(tau, NU), 4)
            u0 = lax.rem(tau, NU)
            rows = pl.ds(pl.multiple_of(pos * S, S), S)
            units = pl.ds(pl.multiple_of(u0 * UC, UC), UC)
            acc[rows, :] += jnp.dot(hid[k], wd[units, :], preferred_element_type=F32)

        @pl.when(k == N - 1)
        def _():
            for i in range(SUB):
                cols = slice(i * UQ, (i + 1) * UQ)

                @pl.when(middle)
                def _():
                    pair_last(i).wait_recv()
                    hid[N - 1, :, cols] = gelu(part[N - 1, :, cols].astype(F32) + pairb[N - 1, :, cols].astype(F32))
                    h_last(i).start()

                @pl.when(end)
                def _():
                    h_last(i).wait_recv()

                units = pl.ds((T0 - 1) * UC + i * UQ, UQ)
                acc[0:S, :] += jnp.dot(hid[N - 1, :, cols], wd[units, :], preferred_element_type=F32)

        @pl.when(k >= WO)
        def _():
            late(k)

        return carry

    def finished(v):
        held = jnp.where(v < 2, 0, jnp.where(v < T0 + 3, v - 1, jnp.where(v < T0 + 9, v, jnp.where(v < T0 + 11, v - 1, v - 2))))
        held = jnp.where(end, v - LE + 1, held)
        return jnp.minimum(jnp.maximum(held, 0), N)

    def step(v, carry):
        @pl.when(v < 2 * NU)
        def _():
            first_terms(v)

        @pl.when(v < N)
        def _():
            share(v)

        @pl.when(v < T0 + 3)
        def _():
            qkv_terms(v)

        @pl.when(jnp.logical_and(v >= T0 + 2, v < T0 + 8))
        def _():
            qkv_share(v)

        lax.fori_loop(finished(v - 1), finished(v), finish, 0)

        @pl.when(jnp.logical_and(v >= T0 + 5, v < T0 + 14))
        def _():
            attend(v)

        return carry

    lax.fori_loop(0, N + LE, step, 0)

    rs_a(0)
    total = x_ref[...].astype(F32) + rows_of(0, par)
    for pos in (1, 2, 3):
        b_copy(pos).wait_recv()
        total = total + rb[pos].astype(F32)
    s_copy(0).wait_recv()
    out_ref[...] = (total + sbuf[0].astype(F32)).astype(BF16)

    for pos in range(4):
        x_sib(pos).wait_send()
        s_copy(pos).wait_send()
    for pos in range(1, 4):
        x_peer(pos).wait_send()
        b_copy(pos).wait_send()
        for q in range(2):
            t_copy(pos, q).wait_send()
    for i, q in mom_pairs:
        m_copy(i, q).wait_send()
    for half in range(2):
        kv_copy(half).wait()
        for kk in range(3):
            q_copy(0, half, 0, 0, kk, inner).wait_send()
        a_copy(0, half, 0, inner).wait_send()

        @pl.when(middle)
        def _():
            for i in range(1, 5):
                a_copy(0, half, i, inner).wait_send()

    def drain(k, carry):
        p_copy(k).wait_send()

        @pl.when(middle)
        def _():
            h_copy(k).wait_send()

        return carry

    lax.fori_loop(0, N - 1, drain, 0)
    for i in range(SUB):
        p_last(i).wait_send()

        @pl.when(middle)
        def _():
            h_last(i).wait_send()


def finish_kernel(a_ref, b_ref, a_out, b_out):
    a_out[...] = a_ref[...]
    b_out[...] = b_ref[...]


def rotary_tables(span, width):
    half = ROT // 2
    inv_freq = np.float32(10000.0) ** (-np.arange(half, dtype=np.float32) * np.float32(2.0) / np.float32(ROT))
    angles = np.arange(span, dtype=np.float32)[:, None] * inv_freq[None, :].astype(np.float32)
    cosine, sine = np.cos(angles), np.sin(angles)
    cos = np.ones((span, width), np.float32)
    front = np.zeros((span, width), np.float32)
    back = np.zeros((span, width), np.float32)
    for low in range(0, width, HD):
        cos[:, low:low + half] = cosine
        cos[:, low + half:low + ROT] = cosine
        front[:, low:low + half] = -sine
        back[:, low + half:low + ROT] = sine
    heads = (np.arange(width)[None, :] // HD == np.arange(8)[:, None]).astype(np.float32)
    return np.stack([cos, front, back]), heads


def fused(
    layer_input, norm_gain_rows, norm_bias_rows, query_key_value_weight, adapter_down_maps,
    adapter_up_maps, output_projection, up_projection, down_projection, prompt_token_length,
    adapter_index, prompt_page_map,
):
    R, C = lax.axis_size("row"), lax.axis_size("col")
    TR, D = layer_input.shape
    T = TR * R
    S = T // C
    W3 = query_key_value_weight.shape[2]
    U = up_projection.shape[1]
    UC = 512
    NU = U // UC
    N = 4 * NU
    wq = jnp.transpose(query_key_value_weight, (1, 0, 2))
    au = jnp.transpose(adapter_up_maps, (0, 2, 1, 3))
    tables = [jnp.asarray(t) for t in rotary_tables(S, W3 // 2)]
    vm = pl.BlockSpec(memory_space=pltpu.VMEM)
    sm = pl.BlockSpec(memory_space=pltpu.SMEM)
    hbm = pl.BlockSpec(memory_space=pl.ANY)
    dma = pltpu.SemaphoreType.DMA
    V = pltpu.VMEM
    HW = W3 // 2
    SUB = 2
    hidden, pages = pl.pallas_call(
        functools.partial(fused_kernel, R, C, NU, UC, 10, SUB),
        out_shape=(
            jax.ShapeDtypeStruct((TR, D), BF16),
            jax.ShapeDtypeStruct((1, 2, S, W3), BF16),
        ),
        in_specs=[hbm] * 11 + [sm] * 3,
        out_specs=(vm, hbm),
        scratch_shapes=[
            V((TR, D), BF16), V((2, D), F32), V((2, D), F32), V((3, S, HW), F32), V((8, HW), F32),
            V(wq.shape, BF16), V(adapter_down_maps.shape, BF16), V(au.shape, BF16),
            V(output_projection.shape, BF16), V(up_projection.shape, BF16), V(down_projection.shape, BF16),
            V((4, 2, TR, D), BF16), V((8, 128), F32), V((C, 2, 8, 128), F32), V((4, 2, 8, 128), F32),
            V((C, S, D), BF16), V((T, D), BF16), V((T, D), BF16), V((C, S, au.shape[2]), BF16),
            V((C, 2, 3, S, HW), BF16), V((2, 3, 2, 3, S, HW), BF16), V((3, S, HW), F32), V((3, S, HW), BF16), V((S, HW), F32),
            V((2, 2, S, HW), BF16),
            V((N, S, UC), BF16), V((N, S, UC), BF16), V((N, S, UC), BF16), V((N, S, UC), BF16),
            V((C, 2, S, HW), BF16), V((T, W3), BF16), V((T, D), F32),
            V((4, TR, D), BF16), V((4, TR, D), BF16), V((4, TR, D), BF16), V((4, TR, D), BF16),
            dma((5,)), dma((2,)), dma((4,)), dma((NU,)), dma((3,)), dma((2, 4)), dma((4, 2)), dma((C, 2)), dma((C, 2)), dma((4, 2)), dma((4, 2)),
            dma((3, 2)), dma((2, 3, 2)), dma((N - 1 + SUB,)), dma((N - 1 + SUB,)), dma((N - 1 + SUB,)), dma((N - 1 + SUB,)),
            dma((5, 2)), dma((C, 2)), dma((4,)), dma((4,)), dma((4,)), dma((4,)),
        ],
        compiler_params=pltpu.CompilerParams(
            collective_id=0, has_side_effects=True, vmem_limit_bytes=63 * 1024 * 1024
        ),
    )(
        layer_input, norm_gain_rows, norm_bias_rows, wq, adapter_down_maps, au,
        output_projection, up_projection, down_projection, *tables,
        prompt_token_length, adapter_index, prompt_page_map,
    )
    return pl.pallas_call(
        finish_kernel,
        out_shape=(
            jax.ShapeDtypeStruct((TR, D), BF16),
            jax.ShapeDtypeStruct((1, 2, S, W3), BF16),
        ),
        in_specs=[vm] * 2,
        out_specs=(vm, vm),
    )(hidden, pages)


def layer(*args):
    rows, weight, up = args[0].shape[0], args[3], args[7]
    R, C = lax.axis_size("row"), lax.axis_size("col")
    span = rows * R // C
    fits = R == 8 and C == 4 and span == 2 * rows and rows % 16 == 0 and rows <= 128
    fits = fits and weight.shape[2] % 128 == 0 and weight.shape[0] % 128 == 0 and up.shape[1] == 6 * 512
    fits = fits and weight.shape[2] % 256 == 0 and weight.shape[2] % (4 * HD) == 0 and weight.shape[2] <= 16 * HD
    return fused(*args) if fits else per_device(*args)


def solution(mesh):
    return jax.shard_map(
        layer,
        mesh=mesh,
        in_specs=(
            P("row", "col"),
            P(None, "col"),
            P(None, "col"),
            P("col", None, "row"),
            P(None, None, "col"),
            P(None, None, None, "row"),
            P("row", "col"),
            P("col", "row"),
            P("row", "col"),
            P(),
            P(),
            P(),
        ),
        out_specs=(P("row", "col"), P("col", None, None, "row")),
        check_vma=False,
    )
```

```python
import functools

import jax
import jax.numpy as jnp
import numpy as np
from jax import lax
from jax.experimental import pallas as pl
from jax.experimental.pallas import tpu as pltpu
from jax.sharding import PartitionSpec as P

MODEL_WIDTH = 6144
HD = 96
ROT = 24


def normalize(hidden_f32, moments, gain_row, bias_row):
    row_mean = (moments[0] / MODEL_WIDTH)[:, None]
    row_var = (moments[1] / MODEL_WIDTH)[:, None] - row_mean * row_mean
    return ((hidden_f32 - row_mean) * lax.rsqrt(row_var + 1e-05) * gain_row + bias_row).astype(
        jnp.bfloat16
    )


def rotate(heads_in, positions):
    half_rot = ROT // 2
    inv_freq = 10000.0 ** (-jnp.arange(half_rot, dtype=jnp.float32) * 2.0 / ROT)
    angles = positions.astype(jnp.float32)[:, None] * inv_freq[None, :]
    cosine = jnp.cos(angles)[:, None, :]
    sine_part = jnp.sin(angles)[:, None, :]
    front_part = heads_in[..., :half_rot]
    back_part = heads_in[..., half_rot:ROT]
    return jnp.concatenate(
        [
            front_part * cosine - back_part * sine_part,
            back_part * cosine + front_part * sine_part,
            heads_in[..., ROT:],
        ],
        axis=-1,
    )


def per_device(
    layer_input,
    norm_gain_rows,
    norm_bias_rows,
    query_key_value_weight,
    adapter_down_maps,
    adapter_up_maps,
    output_projection,
    up_projection,
    down_projection,
    prompt_token_length,
    adapter_index,
    prompt_page_map,
):
    col_width = layer_input.shape[1]
    hidden_f32 = layer_input.astype(jnp.float32)
    moments = lax.psum(
        (jnp.sum(hidden_f32, axis=-1), jnp.sum(hidden_f32 * hidden_f32, axis=-1)), "col"
    )
    normed_attn = normalize(hidden_f32, moments, norm_gain_rows[0], norm_bias_rows[0])
    normed_mlp = normalize(hidden_f32, moments, norm_gain_rows[1], norm_bias_rows[1])
    normed_attn, normed_mlp = (
        lax.all_gather(normed_attn, "row", axis=0, tiled=True),
        lax.all_gather(normed_mlp, "row", axis=0, tiled=True),
    )
    col_count = lax.axis_size("col")
    prompt_span = normed_attn.shape[0] // col_count
    wide_weight = query_key_value_weight.reshape(col_width, -1)
    query_key_value_width = wide_weight.shape[1]
    adapter_wide_term = adapter_up_maps.reshape(
        adapter_up_maps.shape[0], adapter_up_maps.shape[1], query_key_value_width
    )
    token_blocks = normed_attn.reshape(col_count, prompt_span, col_width)
    prompt = lax.axis_index("col")
    tok_slice = token_blocks.reshape(lax.axis_size("col") * prompt_span, col_width)
    base_term = jnp.dot(tok_slice, wide_weight, preferred_element_type=jnp.float32)
    chosen = [adapter_index[i] for i in range(col_count)]
    select_down = jnp.concatenate([lax.dynamic_slice_in_dim(adapter_down_maps, i, 1, 0) for i in chosen])
    select_up = jnp.concatenate([lax.dynamic_slice_in_dim(adapter_wide_term, i, 1, 0) for i in chosen])
    low_rank = jnp.einsum(
        "pld,prd->plr", token_blocks, select_down, preferred_element_type=jnp.float32
    ).astype(jnp.bfloat16)
    extra_term = jnp.einsum("plr,prk->plk", low_rank, select_up, preferred_element_type=jnp.float32)
    qkv_rows = lax.psum_scatter(
        (
            base_term
            + extra_term.reshape(lax.axis_size("col") * prompt_span, query_key_value_width)
        ).astype(jnp.bfloat16),
        "col",
        scatter_dimension=0,
        tiled=True,
    ).astype(jnp.float32)
    local_heads = query_key_value_width // (3 * HD)
    qkv_rows = qkv_rows.reshape(prompt_span, 3, local_heads, HD)
    positions = jnp.arange(prompt_span, dtype=jnp.int32)
    prompt_len = lax.dynamic_slice_in_dim(prompt_token_length, prompt, 1, 0)[0]
    live_mask = positions < prompt_len
    query = rotate(qkv_rows[:, 0], positions).astype(jnp.bfloat16)
    key_rows = rotate(qkv_rows[:, 1], positions).astype(jnp.bfloat16)
    value_rows = qkv_rows[:, 2].astype(jnp.bfloat16)
    zero_key = jnp.zeros_like(key_rows)
    key_rows = jnp.where(live_mask[:, None, None], key_rows, zero_key)
    value_rows = jnp.where(live_mask[:, None, None], value_rows, zero_key)
    scores = jnp.einsum(
        "qhe,khe->hqk", query, key_rows, preferred_element_type=jnp.float32
    ) / jnp.sqrt(jnp.float32(HD))
    allowed = (positions[None, :] <= positions[:, None]) & live_mask[None, :]
    scores = jnp.where(allowed[None, :, :], scores, jnp.float32(-1e30))
    top_score = jnp.max(scores, axis=-1, keepdims=True)
    expo = jnp.exp(scores - top_score)
    probs = (expo / jnp.sum(expo, axis=-1, keepdims=True)).astype(jnp.bfloat16)
    attended = jnp.einsum(
        "hqk,khe->qhe", probs, value_rows, preferred_element_type=jnp.float32
    ).astype(jnp.bfloat16)
    attended = attended.reshape(prompt_span, local_heads * HD)
    page_local = jnp.stack(
        [key_rows.reshape(prompt_span, -1), value_rows.reshape(prompt_span, -1)], axis=0
    )[None]
    target_hit = (prompt_page_map == prompt).astype(jnp.bfloat16)
    kv_pages = jnp.einsum(
        "p,pslk->slk",
        target_hit,
        lax.all_gather(page_local, "col", axis=0, tiled=True),
        preferred_element_type=jnp.float32,
    )[None].astype(jnp.bfloat16)
    tok_slice = normed_mlp
    up_rows = lax.psum_scatter(
        jnp.dot(tok_slice, up_projection, preferred_element_type=jnp.float32).astype(jnp.bfloat16),
        "col",
        scatter_dimension=0,
        tiled=True,
    ).astype(jnp.float32)
    hidden = jax.nn.gelu(up_rows, approximate=False).astype(jnp.bfloat16)
    attn_whole, hidden_whole = (
        lax.all_gather(attended, "col", axis=0, tiled=True),
        lax.all_gather(hidden, "col", axis=0, tiled=True),
    )
    branch = lax.psum_scatter(
        (
            jnp.dot(attn_whole, output_projection, preferred_element_type=jnp.float32)
            + jnp.dot(hidden_whole, down_projection, preferred_element_type=jnp.float32)
        ).astype(jnp.bfloat16),
        "row",
        scatter_dimension=0,
        tiled=True,
    ).astype(jnp.float32)
    new_hidden = (layer_input.astype(jnp.float32) + branch).astype(jnp.bfloat16)
    return (new_hidden, kv_pages)


MESH = pl.DeviceIdType.MESH
F32 = jnp.float32
BF16 = jnp.bfloat16


def remote(src, dst, send_sem, recv_sem, device):
    return pltpu.make_async_remote_copy(
        src_ref=src,
        dst_ref=dst,
        send_sem=send_sem,
        recv_sem=recv_sem,
        device_id=device,
        device_id_type=MESH,
    )


def fused_kernel(
    R, C, NU, UC, LE,
    x_hbm, gain_hbm, bias_hbm, wq_hbm, ad_hbm, au_hbm, wo_hbm, wu_hbm, wd_hbm,
    tab_hbm, hm_hbm, len_ref, aidx_ref, pmap_ref,
    out_ref, kv_hbm,
    x_ref, gain_ref, bias_ref, tab, hm_ref, wq, ad, au, wo, wu, wd,
    xg, mom, momr, st, xn0, xn1, xs, low, qp, rx, qs, qkv, att, kvb,
    part, inp, pairb, hid, attb, ao, acc, sst, sbuf, cb, rb,
    in_sem, kv_sem, w_sem, wu_sem, wq_sem, x_send, x_recv, m_send, m_recv, t_send, t_recv, q_send, q_recv,
    p_send, p_recv, h_send, h_recv, a_send, a_recv, s_send, s_recv, b_send, b_recv,
):
    r = lax.axis_index("row")
    c = lax.axis_index("col")
    par = lax.rem(r, 2)
    chip = lax.div(r, 2)
    sib = r + 1 - 2 * par
    TR, D = x_ref.shape
    S = 2 * TR
    HW = att.shape[1]
    W3 = 2 * HW
    N = 4 * NU
    F0 = 2
    T0 = NU - F0
    QV = F0 + 4
    end = jnp.logical_or(c == 0, c == C - 1)
    middle = jnp.logical_not(end)
    inner = jnp.where(c < C // 2, c + 1, c - 1)
    outer = jnp.where(c == 1, 0, C - 1)
    flip_x = chip + 1 - 2 * lax.rem(chip, 2)
    flip_y = chip + 2 - 4 * lax.div(chip, 2)
    peers = [chip, flip_x, 3 - chip, flip_y]

    def wu_load(u):
        cols = pl.ds(pl.multiple_of(u * UC, UC), UC)
        return pltpu.make_async_copy(wu_hbm.at[:, cols], wu.at[:, cols], wu_sem.at[u])

    def wq_load(j):
        return pltpu.make_async_copy(wq_hbm.at[j], wq.at[j], wq_sem.at[j])

    loads = [
        pltpu.make_async_copy(a, b, w_sem.at[i])
        for i, (a, b) in enumerate([(ad_hbm, ad), (au_hbm, au), (wd_hbm, wd), (wo_hbm, wo)])
    ]
    early = [
        pltpu.make_async_copy(a, b, in_sem.at[i])
        for i, (a, b) in enumerate([(x_hbm, x_ref), (gain_hbm, gain_ref), (bias_hbm, bias_ref), (tab_hbm, tab), (hm_hbm, hm_ref)])
    ]
    for i in range(3):
        early[i].start()
    barrier = pltpu.get_barrier_semaphore()
    for i in range(1, R):
        pl.semaphore_signal(barrier, inc=1, device_id={"row": lax.rem(r + i, R)}, device_id_type=MESH)
    for i in range(1, C):
        for row in (r, sib):
            pl.semaphore_signal(
                barrier, inc=1, device_id={"row": row, "col": lax.rem(c + i, C)}, device_id_type=MESH
            )
    for i in range(NU):
        wu_load((T0 + i) % NU).start()
    for j in range(3):
        wq_load(j).start()
    for ld in loads[:2] + early[3:] + loads[2:]:
        ld.start()
    acc[...] = jnp.zeros_like(acc)
    early[0].wait()

    eye = lax.broadcasted_iota(jnp.int32, (TR, 128), 0) == lax.broadcasted_iota(jnp.int32, (TR, 128), 1)
    line = lax.broadcasted_iota(jnp.int32, (8, 128), 0)
    xf = x_ref[...].astype(F32)
    s1 = jnp.sum(xf, axis=1, keepdims=True)
    s2 = jnp.sum(xf * xf, axis=1, keepdims=True)
    r1 = jnp.sum(jnp.where(eye, s1, 0.0), axis=0, keepdims=True)
    r2 = jnp.sum(jnp.where(eye, s2, 0.0), axis=0, keepdims=True)
    mom[...] = jnp.where(line == 0, r1, jnp.where(line == 1, r2, 0.0))

    pl.semaphore_wait(barrier, R - 1 + 2 * (C - 1))

    def x_sib(pos):
        buf = x_ref if pos == 0 else xg.at[pos, par]
        return remote(buf, xg.at[pos, par], x_send.at[0, pos], x_recv.at[pos, par], {"row": sib})

    def x_from_sib(pos):
        return remote(x_ref, xg.at[pos, 1 - par], x_send.at[0, pos], x_recv.at[pos, 1 - par], {"row": sib})

    def x_peer(pos):
        return remote(x_ref, xg.at[pos, par], x_send.at[1, pos], x_recv.at[pos, par], {"row": 2 * peers[pos] + par})

    def m_copy(i, q):
        row = r if q == 0 else sib
        return remote(
            mom, momr.at[c, par], m_send.at[i, q], m_recv.at[c, par], {"row": row, "col": lax.rem(c + i, C)}
        )

    def m_from(i, q):
        src = lax.rem(c + i, C)
        p = par if q == 0 else 1 - par
        return remote(mom, momr.at[src, p], m_send.at[i, q], m_recv.at[src, p], {"row": sib})

    mom_pairs = [(i, q) for i in range(C) for q in range(2) if (i, q) != (0, 0)]
    for i, q in mom_pairs:
        m_copy(i, q).start()
    x_sib(0).start()
    for pos in (1, 3, 2):
        x_peer(pos).start()
    xg[0, par] = x_ref[...]
    tot0, tot1 = mom[...], jnp.zeros((8, 128), F32)
    for i, q in mom_pairs:
        m_from(i, q).wait_recv()
        src = lax.rem(c + i, C)
        if q == 0:
            tot0 = tot0 + momr[src, par]
        else:
            tot1 = tot1 + momr[src, 1 - par]
    st[0, par] = tot0
    st[0, 1 - par] = tot1

    def t_copy(pos, q):
        row = 2 * peers[pos] + (par if q == 0 else 1 - par)
        return remote(st.at[0, par], st.at[pos, par], t_send.at[pos, q], t_recv.at[pos, par], {"row": row})

    def norm(pos, mlp):
        for q in range(2):
            tile = st[pos, q]
            mean = jnp.sum(jnp.where(eye, tile[0:1, :], 0.0), axis=1, keepdims=True) / MODEL_WIDTH
            square = jnp.sum(jnp.where(eye, tile[1:2, :], 0.0), axis=1, keepdims=True) / MODEL_WIDTH
            z = (xg[pos, q].astype(F32) - mean) * lax.rsqrt(square - mean * mean + 1e-05)
            if mlp:
                xn1[pl.ds(pos * S + q * TR, TR), :] = (z * gain_ref[1:2, :] + bias_ref[1:2, :]).astype(BF16)
            else:
                xn0[peers[pos], pl.ds(q * TR, TR), :] = (z * gain_ref[0:1, :] + bias_ref[0:1, :]).astype(BF16)

    early[1].wait()
    early[2].wait()
    x_from_sib(0).wait_recv()
    norm(0, True)

    inv = []
    for s in range(C):
        v = jnp.int32(0)
        for p in range(1, C):
            v = jnp.where(pmap_ref[p] == s, p, v)
        inv.append(v)
    mine = jnp.int32(0)
    for p in range(1, C):
        mine = jnp.where(pmap_ref[p] == c, p, mine)
    length = len_ref[mine]

    def up(u, lo, rows):
        cols = pl.ds(pl.multiple_of(u * UC, UC), UC)
        return jnp.dot(xn1[pl.ds(lo, rows), :], wu[:, cols], preferred_element_type=F32).astype(BF16)

    def p_copy(k):
        return remote(part.at[k], inp.at[k], p_send.at[k], p_recv.at[k], {"col": inner})

    def pair_copy(k):
        return remote(part.at[k], pairb.at[k], p_send.at[k], h_recv.at[k], {"col": inner})

    def h_copy(k):
        return remote(hid.at[k], hid.at[k], h_send.at[k], h_recv.at[k], {"col": outer})

    def tail_rows(i):
        return pl.ds(pl.multiple_of((par if i >= 2 else 1 - par) * TR, TR), TR)

    def last(buf, i):
        return buf.at[N - 2 + i % 2, tail_rows(i)]

    def p_last(i):
        return remote(last(part, i), last(inp, i), p_send.at[N - 2 + i], p_recv.at[N - 2 + i], {"col": inner})

    def pair_last(i):
        return remote(last(part, i), last(pairb, i), p_send.at[N - 2 + i], h_recv.at[N - 2 + i], {"col": inner})

    def h_last(i):
        return remote(last(hid, i), last(hid, i), h_send.at[N - 2 + i], h_recv.at[N - 2 + i], {"col": outer})

    def q_copy(dest, half, slot, kk, send, device):
        return remote(
            qp.at[dest, half], rx.at[slot, kk, half], q_send.at[send, half], q_recv.at[slot, kk, half], {"col": device}
        )

    def q_wait(slot, kk, half):
        q_copy(0, half, slot, kk, 0, inner).wait_recv()

    def a_copy(s, half, send, device):
        return remote(attb.at[s, half], attb.at[s, half], a_send.at[send, half], a_recv.at[s, half], {"col": device})

    def a_wait(s, half):
        a_copy(s, half, 0, inner).wait_recv()

    def kv_copy(half):
        cols = pl.ds(half * HW, HW)
        return pltpu.make_async_copy(kvb.at[half], kv_hbm.at[0, :, :, cols], kv_sem.at[half])

    def gelu(u):
        return (0.5 * u * (1.0 + lax.erf(u * np.float32(np.sqrt(0.5))))).astype(BF16)

    def s_copy(pos):
        return remote(sst.at[pos], sbuf.at[pos], s_send.at[pos], s_recv.at[pos], {"row": sib})

    def b_copy(pos):
        return remote(cb.at[pos], rb.at[pos], b_send.at[pos], b_recv.at[pos], {"row": 2 * peers[pos] + par})

    def rows_of(pos, q):
        return acc[pl.ds(pl.multiple_of(pos * S + q * TR, TR), TR), :]

    def rs_a(pos):
        sst[pos] = rows_of(pos, 1 - par).astype(BF16)
        s_copy(pos).start()

    def rs_b(pos):
        s_copy(pos).wait_recv()
        cb[pos] = (rows_of(pos, par) + sbuf[pos].astype(F32)).astype(BF16)
        b_copy(pos).start()

    def rot(v):
        return (
            v * tab[0]
            + pltpu.roll(v, HW - ROT // 2, 1) * tab[1]
            + pltpu.roll(v, ROT // 2, 1) * tab[2]
        )

    heads = HW // HD // 2

    def attention(half, a):
        if a == 0:
            if half == 0:
                early[3].wait()
                early[4].wait()

            @pl.when(end)
            def _():
                q_wait(1, 0, half)
                for j in range(3):
                    qs[j] = qp[c, half, j].astype(F32) + rx[1, 0, half, j].astype(F32)

            @pl.when(middle)
            def _():
                q_wait(1, 1, half)
                for j in range(3):
                    qs[j] = qp[c, half, j].astype(F32) + rx[0, 2, half, j].astype(F32) + rx[1, 1, half, j].astype(F32)

            live = lax.broadcasted_iota(jnp.int32, (S, HW), 0) < length
            key = jnp.where(live, rot(qs[1]), 0.0).astype(BF16)
            value = jnp.where(live, qs[2], 0.0).astype(BF16)
            qkv[0] = rot(qs[0]).astype(BF16)
            qkv[1] = key
            qkv[2] = value
            kvb[half, 0] = key
            kvb[half, 1] = value
            kv_copy(half).start()

        qi = lax.broadcasted_iota(jnp.int32, (S, S), 0)
        ki = lax.broadcasted_iota(jnp.int32, (S, S), 1)
        allowed = jnp.logical_and(ki <= qi, ki < length)
        total = jnp.zeros((S, HW), F32) if a == 0 else att[...]
        for h in range(heads):
            mask = hm_ref[a * heads + h:a * heads + h + 1, :]
            scores = lax.dot_general(
                qkv[0] * mask.astype(BF16), qkv[1], (((1,), (1,)), ((), ())), preferred_element_type=F32
            ) / np.float32(np.sqrt(np.float32(HD)))
            scores = jnp.where(allowed, scores, -1e30)
            expo = jnp.exp(scores - jnp.max(scores, axis=1, keepdims=True))
            probs = (expo / jnp.sum(expo, axis=1, keepdims=True)).astype(BF16)
            total = total + jnp.dot(probs, qkv[2], preferred_element_type=F32) * mask
        if a == 0:
            att[...] = total
        else:
            attb[c, half] = total.astype(BF16)
            a_copy(c, half, 0, inner).start()

            @pl.when(middle)
            def _():
                a_copy(c, half, 1, outer).start()

    WO = 17
    q_at = [6, 7, 7, 9, 11, 12]
    att_at = [jnp.where(end, 12, 9), jnp.where(end, 15, 13)]

    def x_ready(pos):
        x_from_sib(pos).wait_recv()
        for q in range(2):
            remote(st.at[0, q], st.at[pos, q], t_send.at[pos, q], t_recv.at[pos, q], {"row": sib}).wait_recv()
        norm(pos, True)

    def first_term(w, carry):
        u = lax.rem(w + T0, NU)

        @pl.when(w == 1)
        def _():
            for pos in range(1, 4):
                for q in range(2):
                    t_copy(pos, q).start()

        @pl.when(w == F0)
        def _():
            @pl.when(middle)
            def _():
                x_peer(1).wait_recv()
                x_sib(1).start()

            x_ready(1)

        @pl.when(w < NU)
        def _():
            wu_load(u).wait()

        ahead = w >= F0 + NU

        @pl.when(jnp.logical_or(w < F0 + NU, w >= F0 + 2 * NU))
        def _():
            lo = jnp.where(jnp.logical_and(w >= F0, w < F0 + NU), S, 0)
            part[jnp.where(ahead, w + NU, w)] = up(u, pl.multiple_of(lo, S), S)

        @pl.when(jnp.logical_and(ahead, w < F0 + 2 * NU))
        def _():
            terms = up(u, 2 * S, 2 * S)
            part[w] = terms[0:S]
            part[w + NU] = terms[S:2 * S]

        return carry

    def first_done(v):
        done = jnp.where(
            end, jnp.where(v < 8, v + 1, 2 * v - 6), jnp.where(v < 0, 0, jnp.where(v < 6, v + 3, 2 * v - 2))
        )
        return jnp.minimum(done, 3 * NU)

    def share(v):
        @pl.when(v < N - 2)
        def _():
            @pl.when(end)
            def _():
                p_copy(v).start()

            @pl.when(middle)
            def _():
                p_copy(v).wait_recv()
                part[v] = (part[v].astype(F32) + inp[v].astype(F32)).astype(BF16)
                pair_copy(v).start()

        for b in range(2):
            @pl.when(v == N - 2 + b)
            def _():
                @pl.when(end)
                def _():
                    for i in (2 * b, 2 * b + 1):
                        p_last(i).start()

                @pl.when(middle)
                def _():
                    for i in (2 * b, 2 * b + 1):
                        p_last(i).wait_recv()
                        mine_last, theirs = last(part, i), last(inp, i)
                        mine_last[...] = (mine_last[...].astype(F32) + theirs[...].astype(F32)).astype(BF16)
                        pair_last(i).start()

    def qkv_terms(v):
        @pl.when(jnp.logical_and(end, v == F0 - 1))
        def _():
            x_peer(1).wait_recv()
            x_sib(1).start()

        @pl.when(v == QV - 3)
        def _():
            for pos in (3, 2):
                x_peer(pos).wait_recv()
                x_sib(pos).start()

        @pl.when(v == QV - 2)
        def _():
            for pos in (3, 2):
                x_ready(pos)
            for pos in range(4):
                norm(pos, False)
            for s in range(C):
                xs[pl.ds(s * S, S), :] = xn0[inv[s]]
            loads[0].wait()
            loads[1].wait()
            for s in range(C):
                low[s] = lax.dot_general(
                    xs[pl.ds(s * S, S), :], ad[aidx_ref[inv[s]]], (((1,), (1,)), ((), ())),
                    preferred_element_type=F32,
                ).astype(BF16)

        @pl.when(v >= QV - 2)
        def _():
            j = v - (QV - 2)
            wq_load(j).wait()
            base = jnp.dot(xs[...], wq[j], preferred_element_type=F32)
            for s in range(C):
                extra = jnp.dot(low[s], au[aidx_ref[inv[s]], j], preferred_element_type=F32)
                term = (base[s * S:(s + 1) * S] + extra).astype(BF16)
                for half in range(2):
                    qp[s, half, j] = term[:, half * HW:(half + 1) * HW]

    def qkv_share(v):
        for m in range(6):
            half, kk = m // 3, m % 3
            dest = jnp.where(c < C // 2, C - 1 - kk, kk)

            @pl.when(v == q_at[m])
            def _():
                @pl.when(end)
                def _():
                    q_copy(dest, half, 0, kk, kk, inner).start()

                @pl.when(middle)
                def _():
                    q_wait(0, kk, half)
                    if kk < 2:
                        for j in range(3):
                            qp[dest, half, j] = (
                                qp[dest, half, j].astype(F32) + rx[0, kk, half, j].astype(F32)
                            ).astype(BF16)
                        q_copy(dest, half, 1, kk, kk, inner).start()
                    if kk == 1:
                        q_wait(1, 0, half)
                        for j in range(3):
                            qp[outer, half, j] = (
                                qp[outer, half, j].astype(F32) + rx[1, 0, half, j].astype(F32)
                            ).astype(BF16)
                        q_copy(outer, half, 1, 0, 2, outer).start()

    def attend(v):
        for half in range(2):
            for a in range(2):
                @pl.when(v == att_at[half] + a)
                def _():
                    attention(half, a)

        @pl.when(middle)
        def _():
            for half, at in enumerate([(13, 12, 14), (16, 16, 18)]):
                @pl.when(v == at[0])
                def _():
                    a_wait(outer, half)
                    a_copy(outer, half, 2, inner).start()

                @pl.when(v == at[1])
                def _():
                    a_wait(inner, half)
                    a_copy(inner, half, 3, outer).start()

                @pl.when(v == at[2])
                def _():
                    a_wait(C - 1 - outer, half)
                    a_copy(C - 1 - outer, half, 4, outer).start()

    def late(k):
        @pl.when(k == WO)
        def _():
            @pl.when(end)
            def _():
                for half in range(2):
                    a_wait(inner, half)
                    a_wait(C - 1 - inner, half)
                    a_wait(C - 1 - c, half)

            loads[3].wait()
            for pos in range(4):
                for half in range(2):
                    ao[pl.ds(pos * S, S), pl.ds(half * HW, HW)] = attb[pmap_ref[peers[pos]], half]
            acc[...] += jnp.dot(ao[...], wo[...], preferred_element_type=F32)
            rs_a(2)
            rs_a(1)

        @pl.when(k == WO + 1)
        def _():
            rs_b(2)
            rs_b(1)

        @pl.when(k == N - T0 - 1)
        def _():
            rs_a(3)

        @pl.when(k == N - T0)
        def _():
            rs_b(3)

    def finish(k, carry):
        @pl.when(k == 0)
        def _():
            loads[2].wait()

        @pl.when(k < N - 2)
        def _():
            @pl.when(middle)
            def _():
                pair_copy(k).wait_recv()
                hid[k] = gelu(part[k].astype(F32) + pairb[k].astype(F32))
                h_copy(k).start()

            @pl.when(end)
            def _():
                h_copy(k).wait_recv()

            tau = k + T0
            pos = lax.rem(lax.div(tau, NU), 4)
            u0 = lax.rem(tau, NU)
            rows = pl.ds(pl.multiple_of(pos * S, S), S)
            units = pl.ds(pl.multiple_of(u0 * UC, UC), UC)
            acc[rows, :] += jnp.dot(hid[k], wd[units, :], preferred_element_type=F32)

        for b in range(2):
            @pl.when(k == N - 2 + b)
            def _():
                for i in (2 * b, 2 * b + 1):
                    @pl.when(middle)
                    def _():
                        pair_last(i).wait_recv()
                        last(hid, i)[...] = gelu(last(part, i)[...].astype(F32) + last(pairb, i)[...].astype(F32))
                        h_last(i).start()

                    @pl.when(end)
                    def _():
                        h_last(i).wait_recv()

                    units = pl.ds((T0 - 2 + i % 2) * UC, UC)
                    acc[tail_rows(i), :] += jnp.dot(last(hid, i)[...], wd[units, :], preferred_element_type=F32)
                if b == 0:
                    rs_a(0)

        @pl.when(k >= WO)
        def _():
            late(k)

        return carry

    def finished(v):
        held = v - 1
        held = jnp.where(end, v - LE + 1, held)
        return jnp.minimum(jnp.maximum(held, 0), N)

    def step(v, carry):
        lax.fori_loop(first_done(v - 1), first_done(v), first_term, 0)

        @pl.when(v < N)
        def _():
            share(v)

        @pl.when(v <= QV)
        def _():
            qkv_terms(v)

        @pl.when(jnp.logical_and(v >= QV, v <= q_at[5]))
        def _():
            qkv_share(v)

        lax.fori_loop(finished(v - 1), finished(v), finish, 0)

        @pl.when(jnp.logical_and(v >= q_at[2] + 2, v < 19))
        def _():
            attend(v)

        return carry

    lax.fori_loop(0, N + LE, step, 0)

    total = x_ref[...].astype(F32) + rows_of(0, par)
    for pos in (1, 2, 3):
        b_copy(pos).wait_recv()
        total = total + rb[pos].astype(F32)
    s_copy(0).wait_recv()
    out_ref[...] = (total + sbuf[0].astype(F32)).astype(BF16)

    for pos in range(4):
        x_sib(pos).wait_send()
        s_copy(pos).wait_send()
    for pos in range(1, 4):
        x_peer(pos).wait_send()
        b_copy(pos).wait_send()
        for q in range(2):
            t_copy(pos, q).wait_send()
    for i, q in mom_pairs:
        m_copy(i, q).wait_send()
    for half in range(2):
        kv_copy(half).wait()
        for kk in range(3):
            q_copy(0, half, 0, 0, kk, inner).wait_send()
        a_copy(0, half, 0, inner).wait_send()

        @pl.when(middle)
        def _():
            for i in range(1, 5):
                a_copy(0, half, i, inner).wait_send()

    def drain(k, carry):
        p_copy(k).wait_send()

        @pl.when(middle)
        def _():
            h_copy(k).wait_send()

        return carry

    lax.fori_loop(0, N - 2, drain, 0)
    for i in range(4):
        p_last(i).wait_send()

        @pl.when(middle)
        def _():
            h_last(i).wait_send()


def rotary_tables(span, width):
    half = ROT // 2
    inv_freq = np.float32(10000.0) ** (-np.arange(half, dtype=np.float32) * np.float32(2.0) / np.float32(ROT))
    angles = np.arange(span, dtype=np.float32)[:, None] * inv_freq[None, :].astype(np.float32)
    cosine, sine = np.cos(angles), np.sin(angles)
    cos = np.ones((span, width), np.float32)
    front = np.zeros((span, width), np.float32)
    back = np.zeros((span, width), np.float32)
    for low in range(0, width, HD):
        cos[:, low:low + half] = cosine
        cos[:, low + half:low + ROT] = cosine
        front[:, low:low + half] = -sine
        back[:, low + half:low + ROT] = sine
    heads = (np.arange(width)[None, :] // HD == np.arange(8)[:, None]).astype(np.float32)
    return np.stack([cos, front, back]), heads


def fused(
    layer_input, norm_gain_rows, norm_bias_rows, query_key_value_weight, adapter_down_maps,
    adapter_up_maps, output_projection, up_projection, down_projection, prompt_token_length,
    adapter_index, prompt_page_map,
):
    R, C = lax.axis_size("row"), lax.axis_size("col")
    TR, D = layer_input.shape
    T = TR * R
    S = T // C
    W3 = query_key_value_weight.shape[2]
    U = up_projection.shape[1]
    UC = 512
    NU = U // UC
    N = 4 * NU
    wq = jnp.transpose(query_key_value_weight, (1, 0, 2))
    au = jnp.transpose(adapter_up_maps, (0, 2, 1, 3))
    tables = [jnp.asarray(t) for t in rotary_tables(S, W3 // 2)]
    vm = pl.BlockSpec(memory_space=pltpu.VMEM)
    sm = pl.BlockSpec(memory_space=pltpu.SMEM)
    hbm = pl.BlockSpec(memory_space=pl.ANY)
    dma = pltpu.SemaphoreType.DMA
    V = pltpu.VMEM
    HW = W3 // 2
    hidden, pages = pl.pallas_call(
        functools.partial(fused_kernel, R, C, NU, UC, 9),
        out_shape=(pltpu.VMEM((TR, D), BF16), pltpu.VMEM((1, 2, S, W3), BF16)),
        in_specs=[hbm] * 11 + [sm] * 3,
        out_specs=(vm, vm),
        scratch_shapes=[
            V((TR, D), BF16), V((2, D), F32), V((2, D), F32), V((3, S, HW), F32), V((8, HW), F32),
            V(wq.shape, BF16), V(adapter_down_maps.shape, BF16), V(au.shape, BF16),
            V(output_projection.shape, BF16), V(up_projection.shape, BF16), V(down_projection.shape, BF16),
            V((4, 2, TR, D), BF16), V((8, 128), F32), V((C, 2, 8, 128), F32), V((4, 2, 8, 128), F32),
            V((C, S, D), BF16), V((T, D), BF16), V((T, D), BF16), V((C, S, au.shape[2]), BF16),
            V((C, 2, 3, S, HW), BF16), V((2, 3, 2, 3, S, HW), BF16), V((3, S, HW), F32), V((3, S, HW), BF16), V((S, HW), F32),
            V((2, 2, S, HW), BF16),
            V((N, S, UC), BF16), V((N, S, UC), BF16), V((N, S, UC), BF16), V((N, S, UC), BF16),
            V((C, 2, S, HW), BF16), V((T, W3), BF16), V((T, D), F32),
            V((4, TR, D), BF16), V((4, TR, D), BF16), V((4, TR, D), BF16), V((4, TR, D), BF16),
            dma((5,)), dma((2,)), dma((4,)), dma((NU,)), dma((3,)), dma((2, 4)), dma((4, 2)), dma((C, 2)), dma((C, 2)), dma((4, 2)), dma((4, 2)),
            dma((3, 2)), dma((2, 3, 2)), dma((N + 2,)), dma((N + 2,)), dma((N + 2,)), dma((N + 2,)),
            dma((5, 2)), dma((C, 2)), dma((4,)), dma((4,)), dma((4,)), dma((4,)),
        ],
        compiler_params=pltpu.CompilerParams(
            collective_id=0, has_side_effects=True, vmem_limit_bytes=62 * 1024 * 1024
        ),
    )(
        layer_input, norm_gain_rows, norm_bias_rows, wq, adapter_down_maps, au,
        output_projection, up_projection, down_projection, *tables,
        prompt_token_length, adapter_index, prompt_page_map,
    )
    return hidden, pages


def layer(*args):
    rows, weight, up = args[0].shape[0], args[3], args[7]
    R, C = lax.axis_size("row"), lax.axis_size("col")
    span = rows * R // C
    fits = R == 8 and C == 4 and span == 2 * rows and rows % 16 == 0 and rows <= 128
    fits = fits and weight.shape[2] % 128 == 0 and weight.shape[0] % 128 == 0 and up.shape[1] == 6 * 512
    fits = fits and weight.shape[2] % 256 == 0 and weight.shape[2] % (4 * HD) == 0 and weight.shape[2] <= 16 * HD
    return fused(*args) if fits else per_device(*args)


def solution(mesh):
    return jax.shard_map(
        layer,
        mesh=mesh,
        in_specs=(
            P("row", "col"),
            P(None, "col"),
            P(None, "col"),
            P("col", None, "row"),
            P(None, None, "col"),
            P(None, None, None, "row"),
            P("row", "col"),
            P("col", "row"),
            P("row", "col"),
            P(),
            P(),
            P(),
        ),
        out_specs=(P("row", "col"), P("col", None, None, "row")),
        check_vma=False,
    )
```

```python
import functools

import jax
import jax.numpy as jnp
import numpy as np
from jax import lax
from jax.experimental import pallas as pl
from jax.experimental.pallas import tpu as pltpu
from jax.sharding import PartitionSpec as P

MODEL_WIDTH = 6144
HD = 96
ROT = 24


def normalize(hidden_f32, moments, gain_row, bias_row):
    row_mean = (moments[0] / MODEL_WIDTH)[:, None]
    row_var = (moments[1] / MODEL_WIDTH)[:, None] - row_mean * row_mean
    return ((hidden_f32 - row_mean) * lax.rsqrt(row_var + 1e-05) * gain_row + bias_row).astype(
        jnp.bfloat16
    )


def rotate(heads_in, positions):
    half_rot = ROT // 2
    inv_freq = 10000.0 ** (-jnp.arange(half_rot, dtype=jnp.float32) * 2.0 / ROT)
    angles = positions.astype(jnp.float32)[:, None] * inv_freq[None, :]
    cosine = jnp.cos(angles)[:, None, :]
    sine_part = jnp.sin(angles)[:, None, :]
    front_part = heads_in[..., :half_rot]
    back_part = heads_in[..., half_rot:ROT]
    return jnp.concatenate(
        [
            front_part * cosine - back_part * sine_part,
            back_part * cosine + front_part * sine_part,
            heads_in[..., ROT:],
        ],
        axis=-1,
    )


def per_device(
    layer_input,
    norm_gain_rows,
    norm_bias_rows,
    query_key_value_weight,
    adapter_down_maps,
    adapter_up_maps,
    output_projection,
    up_projection,
    down_projection,
    prompt_token_length,
    adapter_index,
    prompt_page_map,
):
    col_width = layer_input.shape[1]
    hidden_f32 = layer_input.astype(jnp.float32)
    moments = lax.psum(
        (jnp.sum(hidden_f32, axis=-1), jnp.sum(hidden_f32 * hidden_f32, axis=-1)), "col"
    )
    normed_attn = normalize(hidden_f32, moments, norm_gain_rows[0], norm_bias_rows[0])
    normed_mlp = normalize(hidden_f32, moments, norm_gain_rows[1], norm_bias_rows[1])
    normed_attn, normed_mlp = (
        lax.all_gather(normed_attn, "row", axis=0, tiled=True),
        lax.all_gather(normed_mlp, "row", axis=0, tiled=True),
    )
    col_count = lax.axis_size("col")
    prompt_span = normed_attn.shape[0] // col_count
    wide_weight = query_key_value_weight.reshape(col_width, -1)
    query_key_value_width = wide_weight.shape[1]
    adapter_wide_term = adapter_up_maps.reshape(
        adapter_up_maps.shape[0], adapter_up_maps.shape[1], query_key_value_width
    )
    token_blocks = normed_attn.reshape(col_count, prompt_span, col_width)
    prompt = lax.axis_index("col")
    tok_slice = token_blocks.reshape(lax.axis_size("col") * prompt_span, col_width)
    base_term = jnp.dot(tok_slice, wide_weight, preferred_element_type=jnp.float32)
    chosen = [adapter_index[i] for i in range(col_count)]
    select_down = jnp.concatenate([lax.dynamic_slice_in_dim(adapter_down_maps, i, 1, 0) for i in chosen])
    select_up = jnp.concatenate([lax.dynamic_slice_in_dim(adapter_wide_term, i, 1, 0) for i in chosen])
    low_rank = jnp.einsum(
        "pld,prd->plr", token_blocks, select_down, preferred_element_type=jnp.float32
    ).astype(jnp.bfloat16)
    extra_term = jnp.einsum("plr,prk->plk", low_rank, select_up, preferred_element_type=jnp.float32)
    qkv_rows = lax.psum_scatter(
        (
            base_term
            + extra_term.reshape(lax.axis_size("col") * prompt_span, query_key_value_width)
        ).astype(jnp.bfloat16),
        "col",
        scatter_dimension=0,
        tiled=True,
    ).astype(jnp.float32)
    local_heads = query_key_value_width // (3 * HD)
    qkv_rows = qkv_rows.reshape(prompt_span, 3, local_heads, HD)
    positions = jnp.arange(prompt_span, dtype=jnp.int32)
    prompt_len = lax.dynamic_slice_in_dim(prompt_token_length, prompt, 1, 0)[0]
    live_mask = positions < prompt_len
    query = rotate(qkv_rows[:, 0], positions).astype(jnp.bfloat16)
    key_rows = rotate(qkv_rows[:, 1], positions).astype(jnp.bfloat16)
    value_rows = qkv_rows[:, 2].astype(jnp.bfloat16)
    zero_key = jnp.zeros_like(key_rows)
    key_rows = jnp.where(live_mask[:, None, None], key_rows, zero_key)
    value_rows = jnp.where(live_mask[:, None, None], value_rows, zero_key)
    scores = jnp.einsum(
        "qhe,khe->hqk", query, key_rows, preferred_element_type=jnp.float32
    ) / jnp.sqrt(jnp.float32(HD))
    allowed = (positions[None, :] <= positions[:, None]) & live_mask[None, :]
    scores = jnp.where(allowed[None, :, :], scores, jnp.float32(-1e30))
    top_score = jnp.max(scores, axis=-1, keepdims=True)
    expo = jnp.exp(scores - top_score)
    probs = (expo / jnp.sum(expo, axis=-1, keepdims=True)).astype(jnp.bfloat16)
    attended = jnp.einsum(
        "hqk,khe->qhe", probs, value_rows, preferred_element_type=jnp.float32
    ).astype(jnp.bfloat16)
    attended = attended.reshape(prompt_span, local_heads * HD)
    page_local = jnp.stack(
        [key_rows.reshape(prompt_span, -1), value_rows.reshape(prompt_span, -1)], axis=0
    )[None]
    target_hit = (prompt_page_map == prompt).astype(jnp.bfloat16)
    kv_pages = jnp.einsum(
        "p,pslk->slk",
        target_hit,
        lax.all_gather(page_local, "col", axis=0, tiled=True),
        preferred_element_type=jnp.float32,
    )[None].astype(jnp.bfloat16)
    tok_slice = normed_mlp
    up_rows = lax.psum_scatter(
        jnp.dot(tok_slice, up_projection, preferred_element_type=jnp.float32).astype(jnp.bfloat16),
        "col",
        scatter_dimension=0,
        tiled=True,
    ).astype(jnp.float32)
    hidden = jax.nn.gelu(up_rows, approximate=False).astype(jnp.bfloat16)
    attn_whole, hidden_whole = (
        lax.all_gather(attended, "col", axis=0, tiled=True),
        lax.all_gather(hidden, "col", axis=0, tiled=True),
    )
    branch = lax.psum_scatter(
        (
            jnp.dot(attn_whole, output_projection, preferred_element_type=jnp.float32)
            + jnp.dot(hidden_whole, down_projection, preferred_element_type=jnp.float32)
        ).astype(jnp.bfloat16),
        "row",
        scatter_dimension=0,
        tiled=True,
    ).astype(jnp.float32)
    new_hidden = (layer_input.astype(jnp.float32) + branch).astype(jnp.bfloat16)
    return (new_hidden, kv_pages)


MESH = pl.DeviceIdType.MESH
F32 = jnp.float32
BF16 = jnp.bfloat16


def remote(src, dst, send_sem, recv_sem, device):
    return pltpu.make_async_remote_copy(
        src_ref=src,
        dst_ref=dst,
        send_sem=send_sem,
        recv_sem=recv_sem,
        device_id=device,
        device_id_type=MESH,
    )


def fused_kernel(
    R, C, NU, UC, LE,
    x_hbm, gain_hbm, bias_hbm, wq_hbm, ad_hbm, au_hbm, wo_hbm, wu_hbm, wd_hbm,
    tab_hbm, hm_hbm, len_ref, aidx_ref, pmap_ref,
    out_ref, kv_hbm,
    x_ref, gain_ref, bias_ref, tab, hm_ref, wq, ad, au, wo, wu, wd,
    xg, mom, momr, st, xn0, xn1, xs, low, qp, rx, qs, qkv, att, kvb,
    part, inp, pairb, hid, attb, ao, acc, sst, sbuf, cb, rb,
    in_sem, kv_sem, w_sem, wu_sem, wq_sem, x_send, x_recv, m_send, m_recv, t_send, t_recv, q_send, q_recv,
    p_send, p_recv, h_send, h_recv, a_send, a_recv, s_send, s_recv, b_send, b_recv,
):
    r = lax.axis_index("row")
    c = lax.axis_index("col")
    par = lax.rem(r, 2)
    chip = lax.div(r, 2)
    sib = r + 1 - 2 * par
    TR, D = x_ref.shape
    S = 2 * TR
    HW = att.shape[1]
    W3 = 2 * HW
    N = 4 * NU
    F0 = 2
    T0 = NU - F0
    QV = F0 + 4
    end = jnp.logical_or(c == 0, c == C - 1)
    middle = jnp.logical_not(end)
    inner = jnp.where(c < C // 2, c + 1, c - 1)
    outer = jnp.where(c == 1, 0, C - 1)
    flip_x = chip + 1 - 2 * lax.rem(chip, 2)
    flip_y = chip + 2 - 4 * lax.div(chip, 2)
    peers = [chip, flip_x, 3 - chip, flip_y]

    def wu_load(u):
        cols = pl.ds(pl.multiple_of(u * UC, UC), UC)
        return pltpu.make_async_copy(wu_hbm.at[:, cols], wu.at[:, cols], wu_sem.at[u])

    def wq_load(j):
        return pltpu.make_async_copy(wq_hbm.at[j], wq.at[j], wq_sem.at[j])

    loads = [
        pltpu.make_async_copy(a, b, w_sem.at[i])
        for i, (a, b) in enumerate([(ad_hbm, ad), (au_hbm, au), (wd_hbm, wd), (wo_hbm, wo)])
    ]
    early = [
        pltpu.make_async_copy(a, b, in_sem.at[i])
        for i, (a, b) in enumerate([(x_hbm, x_ref), (gain_hbm, gain_ref), (bias_hbm, bias_ref), (tab_hbm, tab), (hm_hbm, hm_ref)])
    ]
    for i in range(3):
        early[i].start()
    barrier = pltpu.get_barrier_semaphore()
    for i in range(1, R):
        pl.semaphore_signal(barrier, inc=1, device_id={"row": lax.rem(r + i, R)}, device_id_type=MESH)
    for i in range(1, C):
        for row in (r, sib):
            pl.semaphore_signal(
                barrier, inc=1, device_id={"row": row, "col": lax.rem(c + i, C)}, device_id_type=MESH
            )
    wu_load(T0).start()
    early[0].wait()

    eye = lax.broadcasted_iota(jnp.int32, (TR, 128), 0) == lax.broadcasted_iota(jnp.int32, (TR, 128), 1)
    line = lax.broadcasted_iota(jnp.int32, (8, 128), 0)
    xf = x_ref[...].astype(F32)
    s1 = jnp.sum(xf, axis=1, keepdims=True)
    s2 = jnp.sum(xf * xf, axis=1, keepdims=True)
    r1 = jnp.sum(jnp.where(eye, s1, 0.0), axis=0, keepdims=True)
    r2 = jnp.sum(jnp.where(eye, s2, 0.0), axis=0, keepdims=True)
    mom[...] = jnp.where(line == 0, r1, jnp.where(line == 1, r2, 0.0))

    pl.semaphore_wait(barrier, R - 1 + 2 * (C - 1))

    def x_sib(pos):
        buf = x_ref if pos == 0 else xg.at[pos, par]
        return remote(buf, xg.at[pos, par], x_send.at[0, pos], x_recv.at[pos, par], {"row": sib})

    def x_from_sib(pos):
        return remote(x_ref, xg.at[pos, 1 - par], x_send.at[0, pos], x_recv.at[pos, 1 - par], {"row": sib})

    def x_peer(pos):
        return remote(x_ref, xg.at[pos, par], x_send.at[1, pos], x_recv.at[pos, par], {"row": 2 * peers[pos] + par})

    def m_copy(i, q):
        row = r if q == 0 else sib
        return remote(
            mom, momr.at[c, par], m_send.at[i, q], m_recv.at[c, par], {"row": row, "col": lax.rem(c + i, C)}
        )

    def m_from(i, q):
        src = lax.rem(c + i, C)
        p = par if q == 0 else 1 - par
        return remote(mom, momr.at[src, p], m_send.at[i, q], m_recv.at[src, p], {"row": sib})

    mom_pairs = [(i, q) for i in (3, 1, 2) for q in range(2)] + [(0, 1)]
    for i, q in mom_pairs:
        m_copy(i, q).start()
    x_sib(0).start()
    for pos in (1, 3, 2):
        x_peer(pos).start()
    for i in range(1, NU):
        wu_load((T0 + i) % NU).start()
    for j in range(3):
        wq_load(j).start()
    for ld in loads[:2] + early[3:] + loads[2:]:
        ld.start()
    acc[...] = jnp.zeros_like(acc)
    xg[0, par] = x_ref[...]
    tot0, tot1 = mom[...], jnp.zeros((8, 128), F32)
    for i, q in mom_pairs:
        m_from(i, q).wait_recv()
        src = lax.rem(c + i, C)
        if q == 0:
            tot0 = tot0 + momr[src, par]
        else:
            tot1 = tot1 + momr[src, 1 - par]
    st[0, par] = tot0
    st[0, 1 - par] = tot1

    def t_copy(pos, q):
        row = 2 * peers[pos] + (par if q == 0 else 1 - par)
        return remote(st.at[0, par], st.at[pos, par], t_send.at[pos, q], t_recv.at[pos, par], {"row": row})

    def norm(pos, mlp):
        for q in range(2):
            tile = st[pos, q]
            mean = jnp.sum(jnp.where(eye, tile[0:1, :], 0.0), axis=1, keepdims=True) / MODEL_WIDTH
            square = jnp.sum(jnp.where(eye, tile[1:2, :], 0.0), axis=1, keepdims=True) / MODEL_WIDTH
            z = (xg[pos, q].astype(F32) - mean) * lax.rsqrt(square - mean * mean + 1e-05)
            if mlp:
                xn1[pl.ds(pos * S + q * TR, TR), :] = (z * gain_ref[1:2, :] + bias_ref[1:2, :]).astype(BF16)
            else:
                xn0[peers[pos], pl.ds(q * TR, TR), :] = (z * gain_ref[0:1, :] + bias_ref[0:1, :]).astype(BF16)

    early[1].wait()
    early[2].wait()
    x_from_sib(0).wait_recv()
    norm(0, True)

    inv = []
    for s in range(C):
        v = jnp.int32(0)
        for p in range(1, C):
            v = jnp.where(pmap_ref[p] == s, p, v)
        inv.append(v)
    mine = jnp.int32(0)
    for p in range(1, C):
        mine = jnp.where(pmap_ref[p] == c, p, mine)
    length = len_ref[mine]

    def up(u, lo, rows):
        cols = pl.ds(pl.multiple_of(u * UC, UC), UC)
        return jnp.dot(xn1[pl.ds(lo, rows), :], wu[:, cols], preferred_element_type=F32).astype(BF16)

    def p_copy(k):
        return remote(part.at[k], inp.at[k], p_send.at[k], p_recv.at[k], {"col": inner})

    def pair_copy(k):
        return remote(part.at[k], pairb.at[k], p_send.at[k], h_recv.at[k], {"col": inner})

    def h_copy(k):
        return remote(hid.at[k], hid.at[k], h_send.at[k], h_recv.at[k], {"col": outer})

    def tail_rows(i):
        return pl.ds(pl.multiple_of((par if i >= 2 else 1 - par) * TR, TR), TR)

    def last(buf, i):
        return buf.at[N - 2 + i % 2, tail_rows(i)]

    def p_last(i):
        return remote(last(part, i), last(inp, i), p_send.at[N - 2 + i], p_recv.at[N - 2 + i], {"col": inner})

    def pair_last(i):
        return remote(last(part, i), last(pairb, i), p_send.at[N - 2 + i], h_recv.at[N - 2 + i], {"col": inner})

    def h_last(i):
        return remote(last(hid, i), last(hid, i), h_send.at[N - 2 + i], h_recv.at[N - 2 + i], {"col": outer})

    def q_copy(dest, half, slot, kk, send, device):
        return remote(
            qp.at[dest, half], rx.at[slot, kk, half], q_send.at[send, half], q_recv.at[slot, kk, half], {"col": device}
        )

    def q_wait(slot, kk, half):
        q_copy(0, half, slot, kk, 0, inner).wait_recv()

    def a_copy(s, half, send, device):
        return remote(attb.at[s, half], attb.at[s, half], a_send.at[send, half], a_recv.at[s, half], {"col": device})

    def a_wait(s, half):
        a_copy(s, half, 0, inner).wait_recv()

    def kv_copy(half):
        cols = pl.ds(half * HW, HW)
        return pltpu.make_async_copy(kvb.at[half], kv_hbm.at[0, :, :, cols], kv_sem.at[half])

    def gelu(u):
        return (0.5 * u * (1.0 + lax.erf(u * np.float32(np.sqrt(0.5))))).astype(BF16)

    def s_copy(pos):
        return remote(sst.at[pos], sbuf.at[pos], s_send.at[pos], s_recv.at[pos], {"row": sib})

    def b_copy(pos):
        return remote(cb.at[pos], rb.at[pos], b_send.at[pos], b_recv.at[pos], {"row": 2 * peers[pos] + par})

    def rows_of(pos, q):
        return acc[pl.ds(pl.multiple_of(pos * S + q * TR, TR), TR), :]

    def rs_a(pos):
        sst[pos] = rows_of(pos, 1 - par).astype(BF16)
        s_copy(pos).start()

    def rs_b(pos):
        s_copy(pos).wait_recv()
        cb[pos] = (rows_of(pos, par) + sbuf[pos].astype(F32)).astype(BF16)
        b_copy(pos).start()

    def rot(v):
        return (
            v * tab[0]
            + pltpu.roll(v, HW - ROT // 2, 1) * tab[1]
            + pltpu.roll(v, ROT // 2, 1) * tab[2]
        )

    heads = HW // HD // 2

    def attention(half, a):
        if a == 0:
            if half == 0:
                early[3].wait()
                early[4].wait()

            @pl.when(end)
            def _():
                q_wait(1, 0, half)
                for j in range(3):
                    qs[j] = qp[c, half, j].astype(F32) + rx[1, 0, half, j].astype(F32)

            @pl.when(middle)
            def _():
                q_wait(1, 1, half)
                for j in range(3):
                    qs[j] = qp[c, half, j].astype(F32) + rx[0, 2, half, j].astype(F32) + rx[1, 1, half, j].astype(F32)

            live = lax.broadcasted_iota(jnp.int32, (S, HW), 0) < length
            key = jnp.where(live, rot(qs[1]), 0.0).astype(BF16)
            value = jnp.where(live, qs[2], 0.0).astype(BF16)
            qkv[0] = rot(qs[0]).astype(BF16)
            qkv[1] = key
            qkv[2] = value
            kvb[half, 0] = key
            kvb[half, 1] = value
            kv_copy(half).start()

        qi = lax.broadcasted_iota(jnp.int32, (S, S), 0)
        ki = lax.broadcasted_iota(jnp.int32, (S, S), 1)
        allowed = jnp.logical_and(ki <= qi, ki < length)
        total = jnp.zeros((S, HW), F32) if a == 0 else att[...]
        for h in range(heads):
            mask = hm_ref[a * heads + h:a * heads + h + 1, :]
            scores = lax.dot_general(
                qkv[0] * mask.astype(BF16), qkv[1], (((1,), (1,)), ((), ())), preferred_element_type=F32
            ) / np.float32(np.sqrt(np.float32(HD)))
            scores = jnp.where(allowed, scores, -1e30)
            expo = jnp.exp(scores - jnp.max(scores, axis=1, keepdims=True))
            probs = (expo / jnp.sum(expo, axis=1, keepdims=True)).astype(BF16)
            total = total + jnp.dot(probs, qkv[2], preferred_element_type=F32) * mask
        if a == 0:
            att[...] = total
        else:
            attb[c, half] = total.astype(BF16)
            a_copy(c, half, 0, inner).start()

            @pl.when(middle)
            def _():
                a_copy(c, half, 1, outer).start()

    WO = 16
    q_at = [6, 7, 7, 9, 11, 12]
    att_at = [jnp.where(end, 12, 9), jnp.where(end, 14, 13)]

    def x_ready(pos):
        x_from_sib(pos).wait_recv()
        for q in range(2):
            remote(st.at[0, q], st.at[pos, q], t_send.at[pos, q], t_recv.at[pos, q], {"row": sib}).wait_recv()
        norm(pos, True)

    def first_term(w, carry):
        u = lax.rem(w + T0, NU)

        @pl.when(w == 1)
        def _():
            for pos in range(1, 4):
                for q in range(2):
                    t_copy(pos, q).start()

        @pl.when(w == F0)
        def _():
            @pl.when(middle)
            def _():
                x_peer(1).wait_recv()
                x_sib(1).start()

            x_ready(1)

        @pl.when(w < NU)
        def _():
            wu_load(u).wait()

        ahead = w >= F0 + NU

        @pl.when(jnp.logical_or(w < F0 + NU, w >= F0 + 2 * NU))
        def _():
            lo = jnp.where(jnp.logical_and(w >= F0, w < F0 + NU), S, 0)
            part[jnp.where(ahead, w + NU, w)] = up(u, pl.multiple_of(lo, S), S)

        @pl.when(jnp.logical_and(ahead, w < F0 + 2 * NU))
        def _():
            terms = up(u, 2 * S, 2 * S)
            part[w] = terms[0:S]
            part[w + NU] = terms[S:2 * S]

        return carry

    def first_done(v):
        done = jnp.where(
            end, jnp.where(v < 8, v + 1, 2 * v - 6), jnp.where(v < 0, 0, jnp.where(v < 6, v + 3, 2 * v - 2))
        )
        return jnp.minimum(done, 3 * NU)

    def share(v):
        @pl.when(v < N - 2)
        def _():
            @pl.when(end)
            def _():
                p_copy(v).start()

            @pl.when(middle)
            def _():
                p_copy(v).wait_recv()
                part[v] = (part[v].astype(F32) + inp[v].astype(F32)).astype(BF16)
                pair_copy(v).start()

        for b in range(2):
            @pl.when(v == N - 2 + b)
            def _():
                @pl.when(end)
                def _():
                    for i in (2 * b, 2 * b + 1):
                        p_last(i).start()

                @pl.when(middle)
                def _():
                    for i in (2 * b, 2 * b + 1):
                        p_last(i).wait_recv()
                        mine_last, theirs = last(part, i), last(inp, i)
                        mine_last[...] = (mine_last[...].astype(F32) + theirs[...].astype(F32)).astype(BF16)
                        pair_last(i).start()

    def qkv_terms(v):
        @pl.when(jnp.logical_and(end, v == F0 - 1))
        def _():
            x_peer(1).wait_recv()
            x_sib(1).start()

        @pl.when(v == QV - 3)
        def _():
            for pos in (3, 2):
                x_peer(pos).wait_recv()
                x_sib(pos).start()

        @pl.when(v == QV - 2)
        def _():
            for pos in (3, 2):
                x_ready(pos)
            for pos in range(4):
                norm(pos, False)
            for s in range(C):
                xs[pl.ds(s * S, S), :] = xn0[inv[s]]
            loads[0].wait()
            loads[1].wait()
            for s in range(C):
                low[s] = lax.dot_general(
                    xs[pl.ds(s * S, S), :], ad[aidx_ref[inv[s]]], (((1,), (1,)), ((), ())),
                    preferred_element_type=F32,
                ).astype(BF16)

        @pl.when(v >= QV - 2)
        def _():
            j = v - (QV - 2)
            wq_load(j).wait()
            base = jnp.dot(xs[...], wq[j], preferred_element_type=F32)
            for s in range(C):
                extra = jnp.dot(low[s], au[aidx_ref[inv[s]], j], preferred_element_type=F32)
                term = (base[s * S:(s + 1) * S] + extra).astype(BF16)
                for half in range(2):
                    qp[s, half, j] = term[:, half * HW:(half + 1) * HW]

    def qkv_share(v):
        for m in range(6):
            half, kk = m // 3, m % 3
            dest = jnp.where(c < C // 2, C - 1 - kk, kk)

            @pl.when(v == q_at[m])
            def _():
                @pl.when(end)
                def _():
                    q_copy(dest, half, 0, kk, kk, inner).start()

                @pl.when(middle)
                def _():
                    q_wait(0, kk, half)
                    if kk < 2:
                        for j in range(3):
                            qp[dest, half, j] = (
                                qp[dest, half, j].astype(F32) + rx[0, kk, half, j].astype(F32)
                            ).astype(BF16)
                        q_copy(dest, half, 1, kk, kk, inner).start()
                    if kk == 1:
                        q_wait(1, 0, half)
                        for j in range(3):
                            qp[outer, half, j] = (
                                qp[outer, half, j].astype(F32) + rx[1, 0, half, j].astype(F32)
                            ).astype(BF16)
                        q_copy(outer, half, 1, 0, 2, outer).start()

    def attend(v):
        for half in range(2):
            for a in range(2):
                @pl.when(v == att_at[half] + a)
                def _():
                    attention(half, a)

        @pl.when(middle)
        def _():
            for half, at in enumerate([(13, 12, 14), (15, 15, 17)]):
                @pl.when(v == at[0])
                def _():
                    a_wait(outer, half)
                    a_copy(outer, half, 2, inner).start()

                @pl.when(v == at[1])
                def _():
                    a_wait(inner, half)
                    a_copy(inner, half, 3, outer).start()

                @pl.when(v == at[2])
                def _():
                    a_wait(C - 1 - outer, half)
                    a_copy(C - 1 - outer, half, 4, outer).start()

    def late(k):
        @pl.when(k == WO)
        def _():
            @pl.when(end)
            def _():
                for half in range(2):
                    a_wait(inner, half)
                    a_wait(C - 1 - inner, half)
                    a_wait(C - 1 - c, half)

            loads[3].wait()
            for pos in range(4):
                for half in range(2):
                    ao[pl.ds(pos * S, S), pl.ds(half * HW, HW)] = attb[pmap_ref[peers[pos]], half]
            acc[...] += jnp.dot(ao[...], wo[...], preferred_element_type=F32)
            rs_a(2)
            rs_a(1)

        @pl.when(k == WO + 1)
        def _():
            rs_b(2)
            rs_b(1)

        @pl.when(k == N - T0 - 1)
        def _():
            rs_a(3)

        @pl.when(k == N - T0)
        def _():
            rs_b(3)

    def finish(k, carry):
        @pl.when(k == 0)
        def _():
            loads[2].wait()

        @pl.when(k < N - 2)
        def _():
            @pl.when(middle)
            def _():
                pair_copy(k).wait_recv()
                hid[k] = gelu(part[k].astype(F32) + pairb[k].astype(F32))
                h_copy(k).start()

            @pl.when(end)
            def _():
                h_copy(k).wait_recv()

            tau = k + T0
            pos = lax.rem(lax.div(tau, NU), 4)
            u0 = lax.rem(tau, NU)
            rows = pl.ds(pl.multiple_of(pos * S, S), S)
            units = pl.ds(pl.multiple_of(u0 * UC, UC), UC)
            acc[rows, :] += jnp.dot(hid[k], wd[units, :], preferred_element_type=F32)

        for b in range(2):
            @pl.when(k == N - 2 + b)
            def _():
                for i in (2 * b, 2 * b + 1):
                    @pl.when(middle)
                    def _():
                        pair_last(i).wait_recv()
                        last(hid, i)[...] = gelu(last(part, i)[...].astype(F32) + last(pairb, i)[...].astype(F32))
                        h_last(i).start()

                    @pl.when(end)
                    def _():
                        h_last(i).wait_recv()

                    units = pl.ds((T0 - 2 + i % 2) * UC, UC)
                    acc[tail_rows(i), :] += jnp.dot(last(hid, i)[...], wd[units, :], preferred_element_type=F32)
                if b == 0:
                    rs_a(0)

        @pl.when(k >= WO)
        def _():
            late(k)

        return carry

    def finished(v):
        held = v - 1
        held = jnp.where(end, v - LE + 1, held)
        return jnp.minimum(jnp.maximum(held, 0), N)

    def step(v, carry):
        lax.fori_loop(first_done(v - 1), first_done(v), first_term, 0)

        @pl.when(v < N)
        def _():
            share(v)

        @pl.when(v <= QV)
        def _():
            qkv_terms(v)

        @pl.when(jnp.logical_and(v >= QV, v <= q_at[5]))
        def _():
            qkv_share(v)

        lax.fori_loop(finished(v - 1), finished(v), finish, 0)

        @pl.when(jnp.logical_and(v >= q_at[2] + 2, v < 19))
        def _():
            attend(v)

        return carry

    lax.fori_loop(0, N + LE, step, 0)

    total = x_ref[...].astype(F32) + rows_of(0, par)
    for pos in (1, 2, 3):
        b_copy(pos).wait_recv()
        total = total + rb[pos].astype(F32)
    s_copy(0).wait_recv()
    out_ref[...] = (total + sbuf[0].astype(F32)).astype(BF16)

    for pos in range(4):
        x_sib(pos).wait_send()
        s_copy(pos).wait_send()
    for pos in range(1, 4):
        x_peer(pos).wait_send()
        b_copy(pos).wait_send()
        for q in range(2):
            t_copy(pos, q).wait_send()
    for i, q in mom_pairs:
        m_copy(i, q).wait_send()
    for half in range(2):
        kv_copy(half).wait()
        for kk in range(3):
            q_copy(0, half, 0, 0, kk, inner).wait_send()
        a_copy(0, half, 0, inner).wait_send()

        @pl.when(middle)
        def _():
            for i in range(1, 5):
                a_copy(0, half, i, inner).wait_send()

    def drain(k, carry):
        p_copy(k).wait_send()

        @pl.when(middle)
        def _():
            h_copy(k).wait_send()

        return carry

    lax.fori_loop(0, N - 2, drain, 0)
    for i in range(4):
        p_last(i).wait_send()

        @pl.when(middle)
        def _():
            h_last(i).wait_send()


def rotary_tables(span, width):
    half = ROT // 2
    inv_freq = np.float32(10000.0) ** (-np.arange(half, dtype=np.float32) * np.float32(2.0) / np.float32(ROT))
    angles = np.arange(span, dtype=np.float32)[:, None] * inv_freq[None, :].astype(np.float32)
    cosine, sine = np.cos(angles), np.sin(angles)
    cos = np.ones((span, width), np.float32)
    front = np.zeros((span, width), np.float32)
    back = np.zeros((span, width), np.float32)
    for low in range(0, width, HD):
        cos[:, low:low + half] = cosine
        cos[:, low + half:low + ROT] = cosine
        front[:, low:low + half] = -sine
        back[:, low + half:low + ROT] = sine
    heads = (np.arange(width)[None, :] // HD == np.arange(8)[:, None]).astype(np.float32)
    return np.stack([cos, front, back]), heads


def fused(
    layer_input, norm_gain_rows, norm_bias_rows, query_key_value_weight, adapter_down_maps,
    adapter_up_maps, output_projection, up_projection, down_projection, prompt_token_length,
    adapter_index, prompt_page_map,
):
    R, C = lax.axis_size("row"), lax.axis_size("col")
    TR, D = layer_input.shape
    T = TR * R
    S = T // C
    W3 = query_key_value_weight.shape[2]
    U = up_projection.shape[1]
    UC = 512
    NU = U // UC
    N = 4 * NU
    wq = jnp.transpose(query_key_value_weight, (1, 0, 2))
    au = jnp.transpose(adapter_up_maps, (0, 2, 1, 3))
    tables = [jnp.asarray(t) for t in rotary_tables(S, W3 // 2)]
    vm = pl.BlockSpec(memory_space=pltpu.VMEM)
    sm = pl.BlockSpec(memory_space=pltpu.SMEM)
    hbm = pl.BlockSpec(memory_space=pl.ANY)
    dma = pltpu.SemaphoreType.DMA
    V = pltpu.VMEM
    HW = W3 // 2
    hidden, pages = pl.pallas_call(
        functools.partial(fused_kernel, R, C, NU, UC, 9),
        out_shape=(pltpu.VMEM((TR, D), BF16), pltpu.VMEM((1, 2, S, W3), BF16)),
        in_specs=[hbm] * 11 + [sm] * 3,
        out_specs=(vm, vm),
        scratch_shapes=[
            V((TR, D), BF16), V((2, D), F32), V((2, D), F32), V((3, S, HW), F32), V((8, HW), F32),
            V(wq.shape, BF16), V(adapter_down_maps.shape, BF16), V(au.shape, BF16),
            V(output_projection.shape, BF16), V(up_projection.shape, BF16), V(down_projection.shape, BF16),
            V((4, 2, TR, D), BF16), V((8, 128), F32), V((C, 2, 8, 128), F32), V((4, 2, 8, 128), F32),
            V((C, S, D), BF16), V((T, D), BF16), V((T, D), BF16), V((C, S, au.shape[2]), BF16),
            V((C, 2, 3, S, HW), BF16), V((2, 3, 2, 3, S, HW), BF16), V((3, S, HW), F32), V((3, S, HW), BF16), V((S, HW), F32),
            V((2, 2, S, HW), BF16),
            V((N, S, UC), BF16), V((N, S, UC), BF16), V((N, S, UC), BF16), V((N, S, UC), BF16),
            V((C, 2, S, HW), BF16), V((T, W3), BF16), V((T, D), F32),
            V((4, TR, D), BF16), V((4, TR, D), BF16), V((4, TR, D), BF16), V((4, TR, D), BF16),
            dma((5,)), dma((2,)), dma((4,)), dma((NU,)), dma((3,)), dma((2, 4)), dma((4, 2)), dma((C, 2)), dma((C, 2)), dma((4, 2)), dma((4, 2)),
            dma((3, 2)), dma((2, 3, 2)), dma((N + 2,)), dma((N + 2,)), dma((N + 2,)), dma((N + 2,)),
            dma((5, 2)), dma((C, 2)), dma((4,)), dma((4,)), dma((4,)), dma((4,)),
        ],
        compiler_params=pltpu.CompilerParams(
            collective_id=0, has_side_effects=True, vmem_limit_bytes=62 * 1024 * 1024
        ),
    )(
        layer_input, norm_gain_rows, norm_bias_rows, wq, adapter_down_maps, au,
        output_projection, up_projection, down_projection, *tables,
        prompt_token_length, adapter_index, prompt_page_map,
    )
    return hidden, pages


def layer(*args):
    rows, weight, up = args[0].shape[0], args[3], args[7]
    R, C = lax.axis_size("row"), lax.axis_size("col")
    span = rows * R // C
    fits = R == 8 and C == 4 and span == 2 * rows and rows % 16 == 0 and rows <= 128
    fits = fits and weight.shape[2] % 128 == 0 and weight.shape[0] % 128 == 0 and up.shape[1] == 6 * 512
    fits = fits and weight.shape[2] % 256 == 0 and weight.shape[2] % (4 * HD) == 0 and weight.shape[2] <= 16 * HD
    return fused(*args) if fits else per_device(*args)


def solution(mesh):
    return jax.shard_map(
        layer,
        mesh=mesh,
        in_specs=(
            P("row", "col"),
            P(None, "col"),
            P(None, "col"),
            P("col", None, "row"),
            P(None, None, "col"),
            P(None, None, None, "row"),
            P("row", "col"),
            P("col", "row"),
            P("row", "col"),
            P(),
            P(),
            P(),
        ),
        out_specs=(P("row", "col"), P("col", None, None, "row")),
        check_vma=False,
    )
```

```python
import functools

import jax
import jax.numpy as jnp
import numpy as np
from jax import lax
from jax.experimental import pallas as pl
from jax.experimental.pallas import tpu as pltpu
from jax.sharding import PartitionSpec as P

MODEL_WIDTH = 6144
HD = 96
ROT = 24


def normalize(hidden_f32, moments, gain_row, bias_row):
    row_mean = (moments[0] / MODEL_WIDTH)[:, None]
    row_var = (moments[1] / MODEL_WIDTH)[:, None] - row_mean * row_mean
    return ((hidden_f32 - row_mean) * lax.rsqrt(row_var + 1e-05) * gain_row + bias_row).astype(
        jnp.bfloat16
    )


def rotate(heads_in, positions):
    half_rot = ROT // 2
    inv_freq = 10000.0 ** (-jnp.arange(half_rot, dtype=jnp.float32) * 2.0 / ROT)
    angles = positions.astype(jnp.float32)[:, None] * inv_freq[None, :]
    cosine = jnp.cos(angles)[:, None, :]
    sine_part = jnp.sin(angles)[:, None, :]
    front_part = heads_in[..., :half_rot]
    back_part = heads_in[..., half_rot:ROT]
    return jnp.concatenate(
        [
            front_part * cosine - back_part * sine_part,
            back_part * cosine + front_part * sine_part,
            heads_in[..., ROT:],
        ],
        axis=-1,
    )


def per_device(
    layer_input,
    norm_gain_rows,
    norm_bias_rows,
    query_key_value_weight,
    adapter_down_maps,
    adapter_up_maps,
    output_projection,
    up_projection,
    down_projection,
    prompt_token_length,
    adapter_index,
    prompt_page_map,
):
    col_width = layer_input.shape[1]
    hidden_f32 = layer_input.astype(jnp.float32)
    moments = lax.psum(
        (jnp.sum(hidden_f32, axis=-1), jnp.sum(hidden_f32 * hidden_f32, axis=-1)), "col"
    )
    normed_attn = normalize(hidden_f32, moments, norm_gain_rows[0], norm_bias_rows[0])
    normed_mlp = normalize(hidden_f32, moments, norm_gain_rows[1], norm_bias_rows[1])
    normed_attn, normed_mlp = (
        lax.all_gather(normed_attn, "row", axis=0, tiled=True),
        lax.all_gather(normed_mlp, "row", axis=0, tiled=True),
    )
    col_count = lax.axis_size("col")
    prompt_span = normed_attn.shape[0] // col_count
    wide_weight = query_key_value_weight.reshape(col_width, -1)
    query_key_value_width = wide_weight.shape[1]
    adapter_wide_term = adapter_up_maps.reshape(
        adapter_up_maps.shape[0], adapter_up_maps.shape[1], query_key_value_width
    )
    token_blocks = normed_attn.reshape(col_count, prompt_span, col_width)
    prompt = lax.axis_index("col")
    tok_slice = token_blocks.reshape(lax.axis_size("col") * prompt_span, col_width)
    base_term = jnp.dot(tok_slice, wide_weight, preferred_element_type=jnp.float32)
    chosen = [adapter_index[i] for i in range(col_count)]
    select_down = jnp.concatenate([lax.dynamic_slice_in_dim(adapter_down_maps, i, 1, 0) for i in chosen])
    select_up = jnp.concatenate([lax.dynamic_slice_in_dim(adapter_wide_term, i, 1, 0) for i in chosen])
    low_rank = jnp.einsum(
        "pld,prd->plr", token_blocks, select_down, preferred_element_type=jnp.float32
    ).astype(jnp.bfloat16)
    extra_term = jnp.einsum("plr,prk->plk", low_rank, select_up, preferred_element_type=jnp.float32)
    qkv_rows = lax.psum_scatter(
        (
            base_term
            + extra_term.reshape(lax.axis_size("col") * prompt_span, query_key_value_width)
        ).astype(jnp.bfloat16),
        "col",
        scatter_dimension=0,
        tiled=True,
    ).astype(jnp.float32)
    local_heads = query_key_value_width // (3 * HD)
    qkv_rows = qkv_rows.reshape(prompt_span, 3, local_heads, HD)
    positions = jnp.arange(prompt_span, dtype=jnp.int32)
    prompt_len = lax.dynamic_slice_in_dim(prompt_token_length, prompt, 1, 0)[0]
    live_mask = positions < prompt_len
    query = rotate(qkv_rows[:, 0], positions).astype(jnp.bfloat16)
    key_rows = rotate(qkv_rows[:, 1], positions).astype(jnp.bfloat16)
    value_rows = qkv_rows[:, 2].astype(jnp.bfloat16)
    zero_key = jnp.zeros_like(key_rows)
    key_rows = jnp.where(live_mask[:, None, None], key_rows, zero_key)
    value_rows = jnp.where(live_mask[:, None, None], value_rows, zero_key)
    scores = jnp.einsum(
        "qhe,khe->hqk", query, key_rows, preferred_element_type=jnp.float32
    ) / jnp.sqrt(jnp.float32(HD))
    allowed = (positions[None, :] <= positions[:, None]) & live_mask[None, :]
    scores = jnp.where(allowed[None, :, :], scores, jnp.float32(-1e30))
    top_score = jnp.max(scores, axis=-1, keepdims=True)
    expo = jnp.exp(scores - top_score)
    probs = (expo / jnp.sum(expo, axis=-1, keepdims=True)).astype(jnp.bfloat16)
    attended = jnp.einsum(
        "hqk,khe->qhe", probs, value_rows, preferred_element_type=jnp.float32
    ).astype(jnp.bfloat16)
    attended = attended.reshape(prompt_span, local_heads * HD)
    page_local = jnp.stack(
        [key_rows.reshape(prompt_span, -1), value_rows.reshape(prompt_span, -1)], axis=0
    )[None]
    target_hit = (prompt_page_map == prompt).astype(jnp.bfloat16)
    kv_pages = jnp.einsum(
        "p,pslk->slk",
        target_hit,
        lax.all_gather(page_local, "col", axis=0, tiled=True),
        preferred_element_type=jnp.float32,
    )[None].astype(jnp.bfloat16)
    tok_slice = normed_mlp
    up_rows = lax.psum_scatter(
        jnp.dot(tok_slice, up_projection, preferred_element_type=jnp.float32).astype(jnp.bfloat16),
        "col",
        scatter_dimension=0,
        tiled=True,
    ).astype(jnp.float32)
    hidden = jax.nn.gelu(up_rows, approximate=False).astype(jnp.bfloat16)
    attn_whole, hidden_whole = (
        lax.all_gather(attended, "col", axis=0, tiled=True),
        lax.all_gather(hidden, "col", axis=0, tiled=True),
    )
    branch = lax.psum_scatter(
        (
            jnp.dot(attn_whole, output_projection, preferred_element_type=jnp.float32)
            + jnp.dot(hidden_whole, down_projection, preferred_element_type=jnp.float32)
        ).astype(jnp.bfloat16),
        "row",
        scatter_dimension=0,
        tiled=True,
    ).astype(jnp.float32)
    new_hidden = (layer_input.astype(jnp.float32) + branch).astype(jnp.bfloat16)
    return (new_hidden, kv_pages)


MESH = pl.DeviceIdType.MESH
F32 = jnp.float32
BF16 = jnp.bfloat16


def remote(src, dst, send_sem, recv_sem, device):
    return pltpu.make_async_remote_copy(
        src_ref=src,
        dst_ref=dst,
        send_sem=send_sem,
        recv_sem=recv_sem,
        device_id=device,
        device_id_type=MESH,
    )


def fused_kernel(
    R, C, NU, UC, LE,
    x_hbm, gain_hbm, bias_hbm, wq_hbm, ad_hbm, au_hbm, wo_hbm, wu_hbm, wd_hbm,
    tab_hbm, hm_hbm, len_ref, aidx_ref, pmap_ref,
    out_ref, kv_hbm,
    x_ref, gain_ref, bias_ref, tab, hm_ref, wq, ad, au, wo, wu, wd,
    xg, mom, momr, st, xn0, xn1, xs, low, qp, rx, qs, qkv, att, kvb,
    part, inp, pairb, hid, attb, ao, acc, sst, sbuf, cb, rb,
    in_sem, kv_sem, w_sem, wu_sem, wq_sem, x_send, x_recv, m_send, m_recv, t_send, t_recv, q_send, q_recv,
    p_send, p_recv, h_send, h_recv, a_send, a_recv, s_send, s_recv, b_send, b_recv,
):
    r = lax.axis_index("row")
    c = lax.axis_index("col")
    par = lax.rem(r, 2)
    chip = lax.div(r, 2)
    sib = r + 1 - 2 * par
    TR, D = x_ref.shape
    S = 2 * TR
    HW = att.shape[1]
    W3 = 2 * HW
    N = 4 * NU
    F0 = 2
    T0 = NU - F0
    QV = F0 + 4
    end = jnp.logical_or(c == 0, c == C - 1)
    middle = jnp.logical_not(end)
    inner = jnp.where(c < C // 2, c + 1, c - 1)
    outer = jnp.where(c == 1, 0, C - 1)
    flip_x = chip + 1 - 2 * lax.rem(chip, 2)
    flip_y = chip + 2 - 4 * lax.div(chip, 2)
    peers = [chip, flip_x, 3 - chip, flip_y]

    def wu_load(u):
        cols = pl.ds(pl.multiple_of(u * UC, UC), UC)
        return pltpu.make_async_copy(wu_hbm.at[:, cols], wu.at[:, cols], wu_sem.at[u])

    def wq_load(j):
        return pltpu.make_async_copy(wq_hbm.at[j], wq.at[j], wq_sem.at[j])

    loads = [
        pltpu.make_async_copy(a, b, w_sem.at[i])
        for i, (a, b) in enumerate([(ad_hbm, ad), (au_hbm, au), (wd_hbm, wd), (wo_hbm, wo)])
    ]
    early = [
        pltpu.make_async_copy(a, b, in_sem.at[i])
        for i, (a, b) in enumerate([(x_hbm, x_ref), (gain_hbm, gain_ref), (bias_hbm, bias_ref), (tab_hbm, tab), (hm_hbm, hm_ref)])
    ]
    for i in range(3):
        early[i].start()
    barrier = pltpu.get_barrier_semaphore()
    for i in range(1, R):
        pl.semaphore_signal(barrier, inc=1, device_id={"row": lax.rem(r + i, R)}, device_id_type=MESH)
    for i in range(1, C):
        for row in (r, sib):
            pl.semaphore_signal(
                barrier, inc=1, device_id={"row": row, "col": lax.rem(c + i, C)}, device_id_type=MESH
            )
    wu_load(T0).start()
    early[0].wait()

    eye = lax.broadcasted_iota(jnp.int32, (TR, 128), 0) == lax.broadcasted_iota(jnp.int32, (TR, 128), 1)
    line = lax.broadcasted_iota(jnp.int32, (8, 128), 0)
    xf = x_ref[...].astype(F32)
    s1 = jnp.sum(xf, axis=1, keepdims=True)
    s2 = jnp.sum(xf * xf, axis=1, keepdims=True)
    r1 = jnp.sum(jnp.where(eye, s1, 0.0), axis=0, keepdims=True)
    r2 = jnp.sum(jnp.where(eye, s2, 0.0), axis=0, keepdims=True)
    mom[...] = jnp.where(line == 0, r1, jnp.where(line == 1, r2, 0.0))

    pl.semaphore_wait(barrier, R - 1 + 2 * (C - 1))

    def x_sib(pos):
        buf = x_ref if pos == 0 else xg.at[pos, par]
        return remote(buf, xg.at[pos, par], x_send.at[0, pos], x_recv.at[pos, par], {"row": sib})

    def x_from_sib(pos):
        return remote(x_ref, xg.at[pos, 1 - par], x_send.at[0, pos], x_recv.at[pos, 1 - par], {"row": sib})

    def x_peer(pos):
        return remote(x_ref, xg.at[pos, par], x_send.at[1, pos], x_recv.at[pos, par], {"row": 2 * peers[pos] + par})

    def m_copy(i, q):
        row = r if q == 0 else sib
        return remote(
            mom, momr.at[c, par], m_send.at[i, q], m_recv.at[c, par], {"row": row, "col": lax.rem(c + i, C)}
        )

    def m_from(i, q):
        src = lax.rem(c + i, C)
        p = par if q == 0 else 1 - par
        return remote(mom, momr.at[src, p], m_send.at[i, q], m_recv.at[src, p], {"row": sib})

    mom_pairs = [(i, q) for i in (3, 1, 2) for q in range(2)] + [(0, 1)]
    for i, q in mom_pairs:
        m_copy(i, q).start()
    x_sib(0).start()
    for pos in (1, 3, 2):
        x_peer(pos).start()
    for i in range(1, NU):
        wu_load((T0 + i) % NU).start()
    for j in range(3):
        wq_load(j).start()
    for ld in loads[:2] + early[3:] + loads[2:]:
        ld.start()
    acc[...] = jnp.zeros_like(acc)
    xg[0, par] = x_ref[...]
    tot0, tot1 = mom[...], jnp.zeros((8, 128), F32)
    for i, q in mom_pairs:
        m_from(i, q).wait_recv()
        src = lax.rem(c + i, C)
        if q == 0:
            tot0 = tot0 + momr[src, par]
        else:
            tot1 = tot1 + momr[src, 1 - par]
    st[0, par] = tot0
    st[0, 1 - par] = tot1

    def t_copy(pos, q):
        row = 2 * peers[pos] + (par if q == 0 else 1 - par)
        return remote(st.at[0, par], st.at[pos, par], t_send.at[pos, q], t_recv.at[pos, par], {"row": row})

    def norm(pos, attn, mlp):
        for q in range(2):
            tile = st[pos, q]
            mean = jnp.sum(jnp.where(eye, tile[0:1, :], 0.0), axis=1, keepdims=True) / MODEL_WIDTH
            square = jnp.sum(jnp.where(eye, tile[1:2, :], 0.0), axis=1, keepdims=True) / MODEL_WIDTH
            z = (xg[pos, q].astype(F32) - mean) * lax.rsqrt(square - mean * mean + 1e-05)
            if mlp:
                xn1[pl.ds(pos * S + q * TR, TR), :] = (z * gain_ref[1:2, :] + bias_ref[1:2, :]).astype(BF16)
            if attn:
                xn0[peers[pos], pl.ds(q * TR, TR), :] = (z * gain_ref[0:1, :] + bias_ref[0:1, :]).astype(BF16)

    early[1].wait()
    early[2].wait()
    x_from_sib(0).wait_recv()
    norm(0, False, True)

    inv = []
    for s in range(C):
        v = jnp.int32(0)
        for p in range(1, C):
            v = jnp.where(pmap_ref[p] == s, p, v)
        inv.append(v)
    mine = jnp.int32(0)
    for p in range(1, C):
        mine = jnp.where(pmap_ref[p] == c, p, mine)
    length = len_ref[mine]

    def up(u, lo, rows):
        cols = pl.ds(pl.multiple_of(u * UC, UC), UC)
        return jnp.dot(xn1[pl.ds(lo, rows), :], wu[:, cols], preferred_element_type=F32).astype(BF16)

    def p_copy(k):
        return remote(part.at[k], inp.at[k], p_send.at[k], p_recv.at[k], {"col": inner})

    def pair_copy(k):
        return remote(part.at[k], pairb.at[k], p_send.at[k], h_recv.at[k], {"col": inner})

    def h_copy(k):
        return remote(hid.at[k], hid.at[k], h_send.at[k], h_recv.at[k], {"col": outer})

    def tail_rows(i):
        return pl.ds(pl.multiple_of((par if i >= 2 else 1 - par) * TR, TR), TR)

    def last(buf, i):
        return buf.at[N - 2 + i % 2, tail_rows(i)]

    def p_last(i):
        return remote(last(part, i), last(inp, i), p_send.at[N - 2 + i], p_recv.at[N - 2 + i], {"col": inner})

    def pair_last(i):
        return remote(last(part, i), last(pairb, i), p_send.at[N - 2 + i], h_recv.at[N - 2 + i], {"col": inner})

    def h_last(i):
        return remote(last(hid, i), last(hid, i), h_send.at[N - 2 + i], h_recv.at[N - 2 + i], {"col": outer})

    def q_copy(dest, half, slot, kk, send, device):
        return remote(
            qp.at[dest, half], rx.at[slot, kk, half], q_send.at[send, half], q_recv.at[slot, kk, half], {"col": device}
        )

    def q_wait(slot, kk, half):
        q_copy(0, half, slot, kk, 0, inner).wait_recv()

    def a_copy(s, half, send, device):
        return remote(attb.at[s, half], attb.at[s, half], a_send.at[send, half], a_recv.at[s, half], {"col": device})

    def a_wait(s, half):
        a_copy(s, half, 0, inner).wait_recv()

    def kv_copy(half):
        cols = pl.ds(half * HW, HW)
        return pltpu.make_async_copy(kvb.at[half], kv_hbm.at[0, :, :, cols], kv_sem.at[half])

    def gelu(u):
        return (0.5 * u * (1.0 + lax.erf(u * np.float32(np.sqrt(0.5))))).astype(BF16)

    def s_copy(pos):
        return remote(sst.at[pos], sbuf.at[pos], s_send.at[pos], s_recv.at[pos], {"row": sib})

    def b_copy(pos):
        return remote(cb.at[pos], rb.at[pos], b_send.at[pos], b_recv.at[pos], {"row": 2 * peers[pos] + par})

    def rows_of(pos, q):
        return acc[pl.ds(pl.multiple_of(pos * S + q * TR, TR), TR), :]

    def rs_a(pos):
        sst[pos] = rows_of(pos, 1 - par).astype(BF16)
        s_copy(pos).start()

    def rs_b(pos):
        s_copy(pos).wait_recv()
        cb[pos] = (rows_of(pos, par) + sbuf[pos].astype(F32)).astype(BF16)
        b_copy(pos).start()

    def rot(v):
        return (
            v * tab[0]
            + pltpu.roll(v, HW - ROT // 2, 1) * tab[1]
            + pltpu.roll(v, ROT // 2, 1) * tab[2]
        )

    heads = HW // HD // 2

    def attention(half, a):
        if a == 0:
            if half == 0:
                early[3].wait()
                early[4].wait()

            @pl.when(end)
            def _():
                q_wait(1, 0, half)
                for j in range(3):
                    qs[j] = qp[c, half, j].astype(F32) + rx[1, 0, half, j].astype(F32)

            @pl.when(middle)
            def _():
                q_wait(1, 1, half)
                for j in range(3):
                    qs[j] = qp[c, half, j].astype(F32) + rx[0, 2, half, j].astype(F32) + rx[1, 1, half, j].astype(F32)

            live = lax.broadcasted_iota(jnp.int32, (S, HW), 0) < length
            key = jnp.where(live, rot(qs[1]), 0.0).astype(BF16)
            value = jnp.where(live, qs[2], 0.0).astype(BF16)
            qkv[0] = rot(qs[0]).astype(BF16)
            qkv[1] = key
            qkv[2] = value
            kvb[half, 0] = key
            kvb[half, 1] = value
            kv_copy(half).start()

        qi = lax.broadcasted_iota(jnp.int32, (S, S), 0)
        ki = lax.broadcasted_iota(jnp.int32, (S, S), 1)
        allowed = jnp.logical_and(ki <= qi, ki < length)
        total = jnp.zeros((S, HW), F32) if a == 0 else att[...]
        for h in range(heads):
            mask = hm_ref[a * heads + h:a * heads + h + 1, :]
            scores = lax.dot_general(
                qkv[0] * mask.astype(BF16), qkv[1], (((1,), (1,)), ((), ())), preferred_element_type=F32
            ) / np.float32(np.sqrt(np.float32(HD)))
            scores = jnp.where(allowed, scores, -1e30)
            expo = jnp.exp(scores - jnp.max(scores, axis=1, keepdims=True))
            probs = (expo / jnp.sum(expo, axis=1, keepdims=True)).astype(BF16)
            total = total + jnp.dot(probs, qkv[2], preferred_element_type=F32) * mask
        if a == 0:
            att[...] = total
        else:
            attb[c, half] = total.astype(BF16)
            a_copy(c, half, 0, inner).start()

            @pl.when(middle)
            def _():
                a_copy(c, half, 1, outer).start()

    WO = 16
    q_at = [6, 7, 7, 9, 11, 12]
    att_at = [jnp.where(end, 12, 9), jnp.where(end, 14, 13)]

    def x_ready(pos):
        x_from_sib(pos).wait_recv()
        for q in range(2):
            remote(st.at[0, q], st.at[pos, q], t_send.at[pos, q], t_recv.at[pos, q], {"row": sib}).wait_recv()
        norm(pos, pos > 1, True)

    def first_term(w, carry):
        u = lax.rem(w + T0, NU)

        @pl.when(w == 1)
        def _():
            for pos in range(1, 4):
                for q in range(2):
                    t_copy(pos, q).start()

        @pl.when(w == F0)
        def _():
            @pl.when(middle)
            def _():
                x_peer(1).wait_recv()
                x_sib(1).start()

            x_ready(1)

        @pl.when(w < NU)
        def _():
            wu_load(u).wait()

        ahead = w >= F0 + NU

        @pl.when(jnp.logical_or(w < F0 + NU, w >= F0 + 2 * NU))
        def _():
            lo = jnp.where(jnp.logical_and(w >= F0, w < F0 + NU), S, 0)
            part[jnp.where(ahead, w + NU, w)] = up(u, pl.multiple_of(lo, S), S)

        @pl.when(jnp.logical_and(ahead, w < F0 + 2 * NU))
        def _():
            terms = up(u, 2 * S, 2 * S)
            part[w] = terms[0:S]
            part[w + NU] = terms[S:2 * S]

        return carry

    def first_done(v):
        done = jnp.where(
            end, jnp.where(v < 8, v + 1, 2 * v - 6), jnp.where(v < 0, 0, jnp.where(v < 6, v + 3, 2 * v - 2))
        )
        return jnp.minimum(done, 3 * NU)

    def share(v):
        @pl.when(v < N - 2)
        def _():
            @pl.when(end)
            def _():
                p_copy(v).start()

            @pl.when(middle)
            def _():
                p_copy(v).wait_recv()
                part[v] = (part[v].astype(F32) + inp[v].astype(F32)).astype(BF16)
                pair_copy(v).start()

        for b in range(2):
            @pl.when(v == N - 2 + b)
            def _():
                @pl.when(end)
                def _():
                    for i in (2 * b, 2 * b + 1):
                        p_last(i).start()

                @pl.when(middle)
                def _():
                    for i in (2 * b, 2 * b + 1):
                        p_last(i).wait_recv()
                        mine_last, theirs = last(part, i), last(inp, i)
                        mine_last[...] = (mine_last[...].astype(F32) + theirs[...].astype(F32)).astype(BF16)
                        pair_last(i).start()

    def qkv_terms(v):
        @pl.when(jnp.logical_and(end, v == F0 - 1))
        def _():
            x_peer(1).wait_recv()
            x_sib(1).start()

        @pl.when(v == QV - 3)
        def _():
            for pos in (3, 2):
                x_peer(pos).wait_recv()
                x_sib(pos).start()
            for pos in range(2):
                norm(pos, True, False)

        @pl.when(v == QV - 2)
        def _():
            for pos in (3, 2):
                x_ready(pos)
            for s in range(C):
                xs[pl.ds(s * S, S), :] = xn0[inv[s]]
            loads[0].wait()
            loads[1].wait()
            for s in range(C):
                low[s] = lax.dot_general(
                    xs[pl.ds(s * S, S), :], ad[aidx_ref[inv[s]]], (((1,), (1,)), ((), ())),
                    preferred_element_type=F32,
                ).astype(BF16)

        @pl.when(v >= QV - 2)
        def _():
            j = v - (QV - 2)
            wq_load(j).wait()
            base = jnp.dot(xs[...], wq[j], preferred_element_type=F32)
            for s in range(C):
                extra = jnp.dot(low[s], au[aidx_ref[inv[s]], j], preferred_element_type=F32)
                term = (base[s * S:(s + 1) * S] + extra).astype(BF16)
                for half in range(2):
                    qp[s, half, j] = term[:, half * HW:(half + 1) * HW]

    def qkv_share(v):
        for m in range(6):
            half, kk = m // 3, m % 3
            dest = jnp.where(c < C // 2, C - 1 - kk, kk)

            @pl.when(v == q_at[m])
            def _():
                @pl.when(end)
                def _():
                    q_copy(dest, half, 0, kk, kk, inner).start()

                @pl.when(middle)
                def _():
                    q_wait(0, kk, half)
                    if kk < 2:
                        for j in range(3):
                            qp[dest, half, j] = (
                                qp[dest, half, j].astype(F32) + rx[0, kk, half, j].astype(F32)
                            ).astype(BF16)
                        q_copy(dest, half, 1, kk, kk, inner).start()
                    if kk == 1:
                        q_wait(1, 0, half)
                        for j in range(3):
                            qp[outer, half, j] = (
                                qp[outer, half, j].astype(F32) + rx[1, 0, half, j].astype(F32)
                            ).astype(BF16)
                        q_copy(outer, half, 1, 0, 2, outer).start()

    def attend(v):
        for half in range(2):
            for a in range(2):
                @pl.when(v == att_at[half] + a)
                def _():
                    attention(half, a)

        @pl.when(middle)
        def _():
            for half, at in enumerate([(13, 12, 14), (15, 15, 17)]):
                @pl.when(v == at[0])
                def _():
                    a_wait(outer, half)
                    a_copy(outer, half, 2, inner).start()

                @pl.when(v == at[1])
                def _():
                    a_wait(inner, half)
                    a_copy(inner, half, 3, outer).start()

                @pl.when(v == at[2])
                def _():
                    a_wait(C - 1 - outer, half)
                    a_copy(C - 1 - outer, half, 4, outer).start()

    def late(k):
        @pl.when(k == WO)
        def _():
            @pl.when(end)
            def _():
                for half in range(2):
                    a_wait(inner, half)
                    a_wait(C - 1 - inner, half)
                    a_wait(C - 1 - c, half)

            loads[3].wait()
            for pos in range(4):
                for half in range(2):
                    ao[pl.ds(pos * S, S), pl.ds(half * HW, HW)] = attb[pmap_ref[peers[pos]], half]
            acc[...] += jnp.dot(ao[...], wo[...], preferred_element_type=F32)
            rs_a(2)
            rs_a(1)

        @pl.when(k == WO + 1)
        def _():
            rs_b(2)
            rs_b(1)

        @pl.when(k == N - T0 - 1)
        def _():
            rs_a(3)

        @pl.when(k == N - T0)
        def _():
            rs_b(3)

    def finish(k, carry):
        @pl.when(k == 0)
        def _():
            loads[2].wait()

        @pl.when(k < N - 2)
        def _():
            @pl.when(middle)
            def _():
                pair_copy(k).wait_recv()
                hid[k] = gelu(part[k].astype(F32) + pairb[k].astype(F32))
                h_copy(k).start()

            @pl.when(end)
            def _():
                h_copy(k).wait_recv()

            tau = k + T0
            pos = lax.rem(lax.div(tau, NU), 4)
            u0 = lax.rem(tau, NU)
            rows = pl.ds(pl.multiple_of(pos * S, S), S)
            units = pl.ds(pl.multiple_of(u0 * UC, UC), UC)
            acc[rows, :] += jnp.dot(hid[k], wd[units, :], preferred_element_type=F32)

        for b in range(2):
            @pl.when(k == N - 2 + b)
            def _():
                for i in (2 * b, 2 * b + 1):
                    @pl.when(middle)
                    def _():
                        pair_last(i).wait_recv()
                        last(hid, i)[...] = gelu(last(part, i)[...].astype(F32) + last(pairb, i)[...].astype(F32))
                        h_last(i).start()

                    @pl.when(end)
                    def _():
                        h_last(i).wait_recv()

                    units = pl.ds((T0 - 2 + i % 2) * UC, UC)
                    acc[tail_rows(i), :] += jnp.dot(last(hid, i)[...], wd[units, :], preferred_element_type=F32)
                if b == 0:
                    rs_a(0)

        @pl.when(k >= WO)
        def _():
            late(k)

        return carry

    def finished(v):
        held = v - 1
        held = jnp.where(end, v - LE + 1, held)
        return jnp.minimum(jnp.maximum(held, 0), N)

    def step(v, carry):
        lax.fori_loop(first_done(v - 1), first_done(v), first_term, 0)

        @pl.when(v < N)
        def _():
            share(v)

        @pl.when(v <= QV)
        def _():
            qkv_terms(v)

        @pl.when(jnp.logical_and(v >= QV, v <= q_at[5]))
        def _():
            qkv_share(v)

        lax.fori_loop(finished(v - 1), finished(v), finish, 0)

        @pl.when(jnp.logical_and(v >= q_at[2] + 2, v < 19))
        def _():
            attend(v)

        return carry

    lax.fori_loop(0, N + LE, step, 0)

    total = x_ref[...].astype(F32) + rows_of(0, par)
    for pos in (1, 2, 3):
        b_copy(pos).wait_recv()
        total = total + rb[pos].astype(F32)
    s_copy(0).wait_recv()
    out_ref[...] = (total + sbuf[0].astype(F32)).astype(BF16)

    for pos in range(4):
        x_sib(pos).wait_send()
        s_copy(pos).wait_send()
    for pos in range(1, 4):
        x_peer(pos).wait_send()
        b_copy(pos).wait_send()
        for q in range(2):
            t_copy(pos, q).wait_send()
    for i, q in mom_pairs:
        m_copy(i, q).wait_send()
    for half in range(2):
        kv_copy(half).wait()
        for kk in range(3):
            q_copy(0, half, 0, 0, kk, inner).wait_send()
        a_copy(0, half, 0, inner).wait_send()

        @pl.when(middle)
        def _():
            for i in range(1, 5):
                a_copy(0, half, i, inner).wait_send()

    def drain(k, carry):
        p_copy(k).wait_send()

        @pl.when(middle)
        def _():
            h_copy(k).wait_send()

        return carry

    lax.fori_loop(0, N - 2, drain, 0)
    for i in range(4):
        p_last(i).wait_send()

        @pl.when(middle)
        def _():
            h_last(i).wait_send()


def rotary_tables(span, width):
    half = ROT // 2
    inv_freq = np.float32(10000.0) ** (-np.arange(half, dtype=np.float32) * np.float32(2.0) / np.float32(ROT))
    angles = np.arange(span, dtype=np.float32)[:, None] * inv_freq[None, :].astype(np.float32)
    cosine, sine = np.cos(angles), np.sin(angles)
    cos = np.ones((span, width), np.float32)
    front = np.zeros((span, width), np.float32)
    back = np.zeros((span, width), np.float32)
    for low in range(0, width, HD):
        cos[:, low:low + half] = cosine
        cos[:, low + half:low + ROT] = cosine
        front[:, low:low + half] = -sine
        back[:, low + half:low + ROT] = sine
    heads = (np.arange(width)[None, :] // HD == np.arange(8)[:, None]).astype(np.float32)
    return np.stack([cos, front, back]), heads


def fused(
    layer_input, norm_gain_rows, norm_bias_rows, query_key_value_weight, adapter_down_maps,
    adapter_up_maps, output_projection, up_projection, down_projection, prompt_token_length,
    adapter_index, prompt_page_map,
):
    R, C = lax.axis_size("row"), lax.axis_size("col")
    TR, D = layer_input.shape
    T = TR * R
    S = T // C
    W3 = query_key_value_weight.shape[2]
    U = up_projection.shape[1]
    UC = 512
    NU = U // UC
    N = 4 * NU
    wq = jnp.transpose(query_key_value_weight, (1, 0, 2))
    au = jnp.transpose(adapter_up_maps, (0, 2, 1, 3))
    tables = [jnp.asarray(t) for t in rotary_tables(S, W3 // 2)]
    vm = pl.BlockSpec(memory_space=pltpu.VMEM)
    sm = pl.BlockSpec(memory_space=pltpu.SMEM)
    hbm = pl.BlockSpec(memory_space=pl.ANY)
    dma = pltpu.SemaphoreType.DMA
    V = pltpu.VMEM
    HW = W3 // 2
    hidden, pages = pl.pallas_call(
        functools.partial(fused_kernel, R, C, NU, UC, 9),
        out_shape=(pltpu.VMEM((TR, D), BF16), pltpu.VMEM((1, 2, S, W3), BF16)),
        in_specs=[hbm] * 11 + [sm] * 3,
        out_specs=(vm, vm),
        scratch_shapes=[
            V((TR, D), BF16), V((2, D), F32), V((2, D), F32), V((3, S, HW), F32), V((8, HW), F32),
            V(wq.shape, BF16), V(adapter_down_maps.shape, BF16), V(au.shape, BF16),
            V(output_projection.shape, BF16), V(up_projection.shape, BF16), V(down_projection.shape, BF16),
            V((4, 2, TR, D), BF16), V((8, 128), F32), V((C, 2, 8, 128), F32), V((4, 2, 8, 128), F32),
            V((C, S, D), BF16), V((T, D), BF16), V((T, D), BF16), V((C, S, au.shape[2]), BF16),
            V((C, 2, 3, S, HW), BF16), V((2, 3, 2, 3, S, HW), BF16), V((3, S, HW), F32), V((3, S, HW), BF16), V((S, HW), F32),
            V((2, 2, S, HW), BF16),
            V((N, S, UC), BF16), V((N, S, UC), BF16), V((N, S, UC), BF16), V((N, S, UC), BF16),
            V((C, 2, S, HW), BF16), V((T, W3), BF16), V((T, D), F32),
            V((4, TR, D), BF16), V((4, TR, D), BF16), V((4, TR, D), BF16), V((4, TR, D), BF16),
            dma((5,)), dma((2,)), dma((4,)), dma((NU,)), dma((3,)), dma((2, 4)), dma((4, 2)), dma((C, 2)), dma((C, 2)), dma((4, 2)), dma((4, 2)),
            dma((3, 2)), dma((2, 3, 2)), dma((N + 2,)), dma((N + 2,)), dma((N + 2,)), dma((N + 2,)),
            dma((5, 2)), dma((C, 2)), dma((4,)), dma((4,)), dma((4,)), dma((4,)),
        ],
        compiler_params=pltpu.CompilerParams(
            collective_id=0, has_side_effects=True, vmem_limit_bytes=62 * 1024 * 1024
        ),
    )(
        layer_input, norm_gain_rows, norm_bias_rows, wq, adapter_down_maps, au,
        output_projection, up_projection, down_projection, *tables,
        prompt_token_length, adapter_index, prompt_page_map,
    )
    return hidden, pages


def layer(*args):
    rows, weight, up = args[0].shape[0], args[3], args[7]
    R, C = lax.axis_size("row"), lax.axis_size("col")
    span = rows * R // C
    fits = R == 8 and C == 4 and span == 2 * rows and rows % 16 == 0 and rows <= 128
    fits = fits and weight.shape[2] % 128 == 0 and weight.shape[0] % 128 == 0 and up.shape[1] == 6 * 512
    fits = fits and weight.shape[2] % 256 == 0 and weight.shape[2] % (4 * HD) == 0 and weight.shape[2] <= 16 * HD
    return fused(*args) if fits else per_device(*args)


def solution(mesh):
    return jax.shard_map(
        layer,
        mesh=mesh,
        in_specs=(
            P("row", "col"),
            P(None, "col"),
            P(None, "col"),
            P("col", None, "row"),
            P(None, None, "col"),
            P(None, None, None, "row"),
            P("row", "col"),
            P("col", "row"),
            P("row", "col"),
            P(),
            P(),
            P(),
        ),
        out_specs=(P("row", "col"), P("col", None, None, "row")),
        check_vma=False,
    )
```
